1024 devices in a mesh: gx: 32 (over z), gy: 8 (over y_hi, x), gz: 4 (over y_lo, core).
Axes of the slice: x: 4, y: 4 (y_hi: 2, y_lo: 2; y = y_hi * 2 + y_lo), z: 32, core: 2. Of those that a mesh axis runs over, the one named last changes fastest.
Arguments:
- state_grid: float32 [16, 128, 32, 496], P(None, 'gx', 'gy', 'gz'), may hold values from -4 to 4
- diffusivity: float32 [16], replicated, may hold values from 0.1 to 0.5
- prefactor_list: float32 [32], replicated, may hold values from 0.2 to 2
- arrhenius_barrier: float32 [32], replicated, may hold values from 1 to 4
- w_react: float32 [32, 16], replicated, may hold values from -1.5 to 1.5
- stoich_matrix: float32 [16, 32], replicated, may hold values from -1 to 1
- factor_x: float32 [128, 32], P('gx'), may hold values from -1 to 1
- factor_y: float32 [32, 32], P('gy'), may hold values from -1.5 to 1.5
- factor_z: float32 [496, 32], P('gz'), may hold values from -0.375 to 0.375
Outputs:
- advanced: float32 [16, 128, 32, 496], P(None, 'gx', 'gy', 'gz')
- tucker_core: float32 [32, 32, 32, 16], P('gx', 'gy', 'gz')
The draws below stay inside these ranges and needn't reach their ends.
All inputs are finite; a program needn't handle non-finite values.
Results may differ from the reference program's by a relative error of at most 0.0001.
Values sent between devices are 32-bit elements; how exact they have to be, the bound alone decides.
No kernel may reach another device: no remote copies, remote signals or barrier semaphores. Data moves between devices by JAX's collectives and lax.ppermute only.
A program may use at most 32 MiB of HBM per device.

```python
import math
import jax
import jax.numpy as jnp
from jax import lax

NS = 16
NR = 32
R = 32
NX = 128
NY = 32
NZ = 496


def strengthened(result, key, source, target, shards_of, factor):
    def block_of(dim):
        return (jnp.arange(result.shape[dim]) // (result.shape[dim] // shards_of)).reshape((-1,) + (1,) * (result.ndim - 1 - dim))

    first = jax.random.permutation(key, shards_of)[block_of(target)]
    second = (block_of(target) + shards_of // 2) % shards_of
    return jnp.where((block_of(source) == first) | (block_of(source) == second), factor * result, result)


def steps_of(own_key, extent, pieces, smallest, largest):
    def one(dim, parts):
        heights = jax.random.uniform(jax.random.fold_in(jax.random.fold_in(own_key, 6), dim), (parts,), jnp.float32, smallest / len(pieces), largest / len(pieces))
        return jnp.repeat(jnp.exp(heights), extent[dim] // parts).reshape((-1,) + (1,) * (len(extent) - dim - 1))

    factor_of = one(*pieces[0])
    for cut in pieces[1:]:
        factor_of = factor_of * one(*cut)
    return factor_of


def noise(key, dims, width, limit, shards=(), held_as=jnp.bfloat16):
    level = steps_of(key, dims, shards, -0.22, 0.18) if shards else 1.0
    array = jax.random.normal(key, dims, jnp.float32) * width * level
    return jnp.minimum(jnp.maximum(array, -limit), limit).astype(held_as)


def gaussian_with(key, dims, deviation, reach, shards, heavy, kind=jnp.bfloat16):
    result = deviation * jax.random.normal(key, dims, jnp.float32)
    if shards:
        result = result * steps_of(key, dims, shards, -0.22, 0.18)
    return jnp.clip(strengthened(result, jax.random.fold_in(key, 3), *heavy), -reach, reach).astype(kind)


def setup_inputs(seed: int = 0) -> dict:
    seeds = jax.random.split(jax.random.key(seed), 10)
    return {
        "state_grid": noise(seeds[0], (NS, NX, NY, NZ), 1.0, 4.0, ((1, 32), (2, 8), (3, 4)), jnp.float32),
        "diffusivity": jnp.clip(jnp.exp(jax.random.uniform(seeds[1], (NS,), jnp.float32, math.log(0.1), math.log(0.5))), 0.1, 0.5),
        "prefactor_list": jnp.clip(jnp.exp(jax.random.uniform(seeds[2], (NR,), jnp.float32, math.log(0.2), math.log(2.0))), 0.2, 2.0),
        "arrhenius_barrier": jnp.clip(jnp.exp(jax.random.uniform(seeds[3], (NR,), jnp.float32, math.log(1.0), math.log(4.0))), 1.0, 4.0),
        "w_react": noise(seeds[4], (NR, NS), NS ** -0.5, 1.5, (), jnp.float32),
        "stoich_matrix": noise(seeds[5], (NS, NR), NR ** -0.5, 1.0, (), jnp.float32),
        "factor_x": gaussian_with(seeds[6], (NX, R), NX ** -0.5, 1.0, ((0, 32),), (0, 1, 32, 2.75), jnp.float32),
        "factor_y": gaussian_with(seeds[7], (NY, R), NY ** -0.5, 1.5, ((0, 8),), (0, 1, 8, 2.0), jnp.float32),
        "factor_z": gaussian_with(seeds[8], (NZ, R), NZ ** -0.5, 0.375, ((0, 4),), (0, 1, 4, 2.0), jnp.float32),
    }


def tendency(state_grid, diffusivity, prefactor_list, arrhenius_barrier, w_react, stoich_matrix):
    bordered_field = jnp.pad(state_grid, ((0, 0), (2, 2), (2, 2), (2, 2)))
    heat_level_grid = 1.5 + jnp.tanh(bordered_field[0])
    scale_multiplier = jnp.power(heat_level_grid / 2.5, 0.7)
    shape = bordered_field.shape

    def one_species(pair):
        layer, coeff = pair
        transport_coeff_value = coeff * scale_multiplier
        summed = jnp.zeros((shape[1] - 4, shape[2] - 4, shape[3] - 4), jnp.float32)
        for axis_dim in (0, 1, 2):
            length = layer.shape[axis_dim]
            gradient = 0.5 * (lax.slice_in_dim(layer, 2, length, axis=axis_dim) - lax.slice_in_dim(layer, 0, length - 2, axis=axis_dim))
            flux_part = lax.slice_in_dim(transport_coeff_value, 1, length - 1, axis=axis_dim) * gradient
            divergence = 0.5 * (lax.slice_in_dim(flux_part, 2, length - 2, axis=axis_dim) - lax.slice_in_dim(flux_part, 0, length - 4, axis=axis_dim))
            for other in (0, 1, 2):
                if other != axis_dim:
                    divergence = lax.slice_in_dim(divergence, 2, layer.shape[other] - 2, axis=other)
            summed = summed + divergence
        return summed

    diffusive_term = lax.map(one_species, (bordered_field, diffusivity))
    core_heat_level = heat_level_grid[2:-2, 2:-2, 2:-2]

    def react(source, pack):
        weight_line, s_col, basis_matrix, heat_content = pack
        reaction_speed = basis_matrix * jnp.exp(-heat_content / core_heat_level) * jnp.tensordot(weight_line, state_grid, axes=1, precision=lax.Precision.HIGHEST)
        return source + s_col[:, None, None, None] * reaction_speed[None], None

    source, unused = lax.scan(react, jnp.zeros_like(state_grid), (w_react, stoich_matrix.T, prefactor_list, arrhenius_barrier))
    return diffusive_term + source


def reference(state_grid, diffusivity, prefactor_list, arrhenius_barrier, w_react, stoich_matrix, factor_x, factor_y, factor_z):
    args = (diffusivity, prefactor_list, arrhenius_barrier, w_react, stoich_matrix)
    first = state_grid + tendency(state_grid, *args)
    second_term = 0.75 * state_grid + 0.25 * (first + tendency(first, *args))
    advanced = (1.0 / 3.0) * state_grid + (2.0 / 3.0) * (second_term + tendency(second_term, *args))
    highest = lax.Precision.HIGHEST
    partial_value = jnp.einsum('sxyz,xa->asyz', advanced, factor_x, precision=highest)
    partial_value = jnp.einsum('asyz,yb->absz', partial_value, factor_y, precision=highest)
    tucker_core = jnp.einsum('absz,zc->abcs', partial_value, factor_z, precision=highest)
    return advanced, tucker_core
```

```python
import jax
import jax.numpy as jnp
from jax import lax
from jax.experimental import pallas as pl
from jax.experimental.pallas import tpu as pltpu
from jax.sharding import PartitionSpec as P

NS, NR, NX, NY, NZ = 16, 32, 4, 4, 124
PLANES = NX * NY
LANES = 128
NB, NC = 4, 8
HIGH = lax.Precision.HIGHEST
F32 = jnp.float32


def vmem(n):
    return [pl.BlockSpec(memory_space=pltpu.VMEM)] * n


def smem(n):
    return [pl.BlockSpec(memory_space=pltpu.SMEM)] * n


def shaped(*shape):
    return jax.ShapeDtypeStruct(shape, F32)


def lanes_of(shape):
    return lax.broadcasted_iota(jnp.int32, shape, len(shape) - 1)


FIELD = (PLANES, NS, LANES)
FACE = (8, NS, LANES)


def put_faces(k, plane, faces):
    x_low, x_high, y_low, y_high = faces
    x, y = divmod(k, NY)
    if x < 2:
        x_low[x * NY + y] = plane
    else:
        x_high[(x - 2) * NY + y] = plane
    if y < 2:
        y_low[x * 2 + y] = plane
    else:
        y_high[x * 2 + y - 2] = plane
    return pltpu.roll(plane, (8 * k - 122) % LANES, 1)


def setup_kernel(diff, pref, barrier, w_react, factor_y, factor_z, w_out, diff_out, bar_out, fz_out, fy_out, fz_pad):
    for s in range(NS):
        diff_out[s : s + 1, :] = jnp.full((1, LANES), 0.25 * diff[s], F32)
    for r in range(NR):
        bar_out[r : r + 1, :] = jnp.full((1, LANES), -barrier[r], F32)
        w_out[r : r + 1, :] = pref[r] * w_react[r : r + 1, :]
    fz_pad[...] = jnp.zeros(fz_pad.shape, F32)
    fz_pad[0:NZ, :] = factor_z[...]
    cores = factor_z.shape[1]
    wide = fz_out.shape[1]
    row = lax.broadcasted_iota(jnp.int32, (cores, wide), 0)
    lane = lanes_of((cores, wide))
    pick = (row == (lane // LANES) * NC + lane % NC).astype(F32)
    fz_out[...] = jnp.dot(fz_pad[...], pick, precision=HIGH, preferred_element_type=F32)
    cores = factor_y.shape[1]
    wide = fy_out.shape[1]
    row = lax.broadcasted_iota(jnp.int32, (cores, wide), 0)
    lane = lanes_of((cores, wide))
    pick = (row == (lane // LANES) * NB + (lane // NC) % NB).astype(F32)
    fy_out[...] = jnp.dot(factor_y[...], pick, precision=HIGH, preferred_element_type=F32)


def enter_kernel(state, field, x_low, x_high, y_low, y_high, packed):
    lane = lanes_of((NS, LANES))
    joined = jnp.zeros((NS, LANES), F32)
    for k in range(PLANES):
        x, y = divmod(k, NY)
        plane = jnp.concatenate([state[:, x, y, :], jnp.zeros((NS, LANES - NZ), F32)], axis=1)
        field[k] = plane
        rolled = put_faces(k, plane, (x_low, x_high, y_low, y_high))
        joined = jnp.where(lane // 8 == k, rolled, joined)
    packed[...] = joined


def source_kernel(rates, *refs):
    c_state, c_now = rates
    if c_state:
        state, field, w, bar, stoich, base, inverse = refs
    else:
        field, w, bar, stoich, base, inverse = refs
        state = None
    inverse[...] = 1.0 / (1.5 + jnp.tanh(field[:, 0, :]))
    cells = jnp.concatenate([field[k] for k in range(PLANES)], axis=1)
    speed = jnp.dot(w[...], cells, precision=HIGH, preferred_element_type=F32)
    heat = jnp.concatenate(
        [jnp.exp(bar[...] * jnp.broadcast_to(inverse[k : k + 1, :], (NR, LANES))) for k in range(PLANES)], axis=1
    )
    source = jnp.dot(stoich[...], speed * heat, precision=HIGH, preferred_element_type=F32)
    for k in range(PLANES):
        value = c_now * (field[k] + source[:, k * LANES : (k + 1) * LANES])
        if state is not None:
            value = value + c_state * state[k]
        base[k] = value


def scale_of(rows):
    return jnp.exp(0.7 * jnp.log((1.5 + jnp.tanh(rows)) / 2.5))


def advance(c_now, base, field, diff, x_before, x_after, y_before, y_after, z_before, z_after, full, own_k, side_k, emit):
    lane = lanes_of((NS, LANES))
    z_halo = jnp.where(lane % 8 < 2, pltpu.roll(z_after[...], LANES - 6, 1), pltpu.roll(z_before[...], 2, 1))
    for k in range(PLANES):
        full[k] = jnp.where(lane < NZ, field[k], pltpu.roll(z_halo, (NZ - 8 * k) % LANES, 1))
    own_k[...] = scale_of(full[:, 0, :])
    for i in range(4):
        side_k[i : i + 1, :] = x_before[4 + i, 0:1, :]
        side_k[4 + i : 5 + i, :] = x_after[i, 0:1, :]
        side_k[8 + i : 9 + i, :] = y_before[2 * i + 1, 0:1, :]
        side_k[12 + i : 13 + i, :] = y_after[2 * i, 0:1, :]
    side_k[...] = scale_of(side_k[...])
    weight = c_now * diff[...]

    def wide(row):
        return jnp.broadcast_to(row, (NS, LANES))

    def k_at(x, y):
        if x < 0:
            return wide(side_k[y : y + 1, :])
        if x >= NX:
            return wide(side_k[4 + y : 5 + y, :])
        if y < 0:
            return wide(side_k[8 + x : 9 + x, :])
        if y >= NY:
            return wide(side_k[12 + x : 13 + x, :])
        k = x * NY + y
        return wide(own_k[k : k + 1, :])

    def y_at(x, y):
        if x < 0:
            return x_before[(x + 2) * NY + y]
        if x >= NX:
            return x_after[(x - NX) * NY + y]
        if y < 0:
            return y_before[x * 2 + y + 2]
        if y >= NY:
            return y_after[x * 2 + y - NY]
        return full[x * NY + y]

    for k in range(PLANES):
        x, y = divmod(k, NY)
        here = full[k]
        total = k_at(x + 1, y) * (y_at(x + 2, y) - here) - k_at(x - 1, y) * (here - y_at(x - 2, y))
        total = total + (k_at(x, y + 1) * (y_at(x, y + 2) - here) - k_at(x, y - 1) * (here - y_at(x, y - 2)))
        row = own_k[k : k + 1, :]
        after = wide(pltpu.roll(row, LANES - 1, 1))
        before = wide(pltpu.roll(row, 1, 1))
        total = total + (after * (pltpu.roll(here, LANES - 2, 1) - here) - before * (here - pltpu.roll(here, 2, 1)))
        emit(k, base[k] + weight * total)


def section_kernel(c_now, *refs):
    ins, (field, x_low, x_high, y_low, y_high, packed), scratch = refs[:9], refs[9:15], refs[15:]
    lane = lanes_of((NS, LANES))
    packed[...] = jnp.zeros((NS, LANES), F32)

    def emit(k, plane):
        field[k] = plane
        rolled = put_faces(k, plane, (x_low, x_high, y_low, y_high))
        packed[...] = jnp.where(lane // 8 == k, rolled, packed[...])

    advance(c_now, *ins, *scratch, emit)


def last_kernel(c_now, *refs):
    ins, (fz, fy), (advanced, parts), scratch = refs[:9], refs[9:11], refs[11:13], refs[13:16]
    rows = refs[16]
    lane = lanes_of((NS, LANES))

    def emit(k, plane):
        x, y = divmod(k, NY)
        advanced[:, x, y, :] = plane[:, :NZ]
        rows[k * NS : (k + 1) * NS, :] = jnp.where(lane < NZ, plane, 0.0)

    advance(c_now, *ins, *scratch, emit)
    along_z = jnp.dot(rows[...], fz[...], precision=HIGH, preferred_element_type=F32)
    n_z = fz.shape[1] // LANES
    n_y = fy.shape[1] // LANES
    for g in range(n_z):
        by_y = []
        for y in range(NY):
            value = along_z[y * NS : (y + 1) * NS, g * LANES : (g + 1) * LANES]
            for x in range(1, NX):
                k = x * NY + y
                value = jnp.where(
                    lane // 32 == x, along_z[k * NS : (k + 1) * NS, g * LANES : (g + 1) * LANES], value
                )
            by_y.append(value)
        for j in range(n_y):
            total = fy[0:1, j * LANES : (j + 1) * LANES] * by_y[0]
            for y in range(1, NY):
                total = total + fy[y : y + 1, j * LANES : (j + 1) * LANES] * by_y[y]
            parts[j * n_z + g] = total


def middle_kernel(factor_x, parts, out):
    count = parts.shape[0]
    terms = [parts[i] for i in range(count)]
    while len(terms) > 1:
        terms = [terms[i] + terms[i + 1] for i in range(0, len(terms), 2)]
    total = terms[0]
    lane = lanes_of((4, LANES))
    by_x = []
    for x in range(NX):
        value = jnp.zeros((4, LANES), F32)
        for low in range(4):
            rolled = total[4 * low : 4 * low + 4, :]
            if low != x:
                rolled = pltpu.roll(rolled, (32 * (low - x)) % LANES, 1)
            value = jnp.where(lane // 32 == low, rolled, value)
        by_x.append(value)
    for a in range(out.shape[0]):
        value = factor_x[0, a] * by_x[0]
        for x in range(1, NX):
            value = value + factor_x[x, a] * by_x[x]
        out[a] = value


def final_kernel(parts, out, rows):
    count = parts.shape[0]
    terms = [parts[i] for i in range(count)]
    while len(terms) > 1:
        terms = [terms[i] + terms[i + 1] for i in range(0, len(terms), 2)]
    total = terms[0]
    for low in range(4):
        piece = total if low == 0 else pltpu.roll(total, LANES - 32 * low, 1)
        rows[4 * low : 4 * low + 4, :] = piece
    turned = jnp.transpose(rows[...])
    for b in range(NB):
        out[0, b] = turned[b * NC : (b + 1) * NC, :]


def shifted(faces):
    x_low, x_high, y_low, y_high, packed = faces

    def up(value, axis):
        count = lax.axis_size(axis)
        return lax.ppermute(value, axis, [(i, i + 1) for i in range(count - 1)])

    def down(value, axis):
        count = lax.axis_size(axis)
        return lax.ppermute(value, axis, [(i + 1, i) for i in range(count - 1)])

    y_before, y_after = up(y_high, "gy"), down(y_low, "gy")
    x_before, x_after = up(x_high, "gx"), down(x_low, "gx")
    z_before, z_after = up(packed, "gz"), down(packed, "gz")
    return x_before, x_after, y_before, y_after, z_before, z_after


HALO_SCRATCH = [pltpu.VMEM(FIELD, F32), pltpu.VMEM((PLANES, LANES), F32), pltpu.VMEM((16, LANES), F32)]
FACES = [shaped(*FIELD), shaped(*FACE), shaped(*FACE), shaped(*FACE), shaped(*FACE), shaped(NS, LANES)]


def local(state_grid, diffusivity, prefactor_list, arrhenius_barrier, w_react, stoich_matrix, factor_x, factor_y, factor_z):
    n_x, n_y, n_z = (lax.axis_size(axis) for axis in ("gx", "gy", "gz"))
    w, diff, bar, fz, fy = pl.pallas_call(
        setup_kernel,
        name="setup",
        out_shape=[shaped(NR, NS), shaped(NS, LANES), shaped(NR, LANES), shaped(LANES, n_z * LANES), shaped(NY, n_y * LANES)],
        in_specs=smem(3) + vmem(3),
        out_specs=vmem(5),
        scratch_shapes=[pltpu.VMEM((LANES, factor_z.shape[1]), F32)],
    )(diffusivity, prefactor_list, arrhenius_barrier, w_react, factor_y, factor_z)

    state, *faces = pl.pallas_call(
        enter_kernel, name="enter", out_shape=FACES, in_specs=vmem(1), out_specs=vmem(6)
    )(state_grid)

    def base_of(c_state, c_now, field):
        ins = ([state] if c_state else []) + [field, w, bar, stoich_matrix]
        return pl.pallas_call(
            lambda *refs: source_kernel((c_state, c_now), *refs),
            name="source",
            out_shape=shaped(*FIELD),
            in_specs=vmem(len(ins)),
            out_specs=vmem(1)[0],
            scratch_shapes=[pltpu.VMEM((PLANES, LANES), F32)],
        )(*ins)

    field = state
    for c_state, c_now in ((0.0, 1.0), (0.75, 0.25)):
        halos = shifted(faces)
        base = base_of(c_state, c_now, field)
        field, *faces = pl.pallas_call(
            lambda *refs, c_now=c_now: section_kernel(c_now, *refs),
            name="section",
            out_shape=FACES,
            in_specs=vmem(9),
            out_specs=vmem(6),
            scratch_shapes=HALO_SCRATCH,
        )(base, field, diff, *halos)
    c_state, c_now = 1.0 / 3.0, 2.0 / 3.0
    halos = shifted(faces)
    base = base_of(c_state, c_now, field)
    advanced, parts = pl.pallas_call(
        lambda *refs: last_kernel(c_now, *refs),
        name="last",
        out_shape=[shaped(NS, NX, NY, NZ), shaped(n_y * n_z, NS, LANES)],
        in_specs=vmem(11),
        out_specs=vmem(2),
        scratch_shapes=HALO_SCRATCH + [pltpu.VMEM((PLANES * NS, LANES), F32)],
    )(base, field, diff, *halos, fz, fy)
    parts = lax.all_to_all(parts, ("gy", "gz"), 0, 0, tiled=True)
    parts = pl.pallas_call(
        middle_kernel, name="middle", out_shape=shaped(n_x, 4, LANES), in_specs=smem(1) + vmem(1), out_specs=vmem(1)[0]
    )(factor_x, parts)
    parts = lax.all_to_all(parts, "gx", 0, 0, tiled=True)
    tucker_core = pl.pallas_call(
        final_kernel,
        name="final",
        out_shape=shaped(1, NB, NC, NS),
        in_specs=vmem(1),
        out_specs=vmem(1)[0],
        scratch_shapes=[pltpu.VMEM((NS, LANES), F32)],
    )(parts)
    return advanced, tucker_core


def solution(mesh):
    placed = (P(None, "gx", "gy", "gz"), P(), P(), P(), P(), P(), P("gx", None), P("gy", None), P("gz", None))
    return jax.shard_map(
        local,
        mesh=mesh,
        in_specs=placed,
        out_specs=(P(None, "gx", "gy", "gz"), P("gx", "gy", "gz", None)),
        check_vma=False,
    )
```

```python
import jax
import jax.numpy as jnp
from jax import lax
from jax.experimental import pallas as pl
from jax.experimental.pallas import tpu as pltpu
from jax.sharding import PartitionSpec as P

NS, NR, NX, NY, NZ = 16, 32, 4, 4, 124
PLANES = NX * NY
LANES = 128
NB, NC = 4, 8
HIGH = lax.Precision.HIGHEST
F32 = jnp.float32


def vmem(n):
    return [pl.BlockSpec(memory_space=pltpu.VMEM)] * n


def smem(n):
    return [pl.BlockSpec(memory_space=pltpu.SMEM)] * n


def shaped(*shape):
    return jax.ShapeDtypeStruct(shape, F32)


def lanes_of(shape):
    return lax.broadcasted_iota(jnp.int32, shape, len(shape) - 1)


FIELD = (PLANES, NS, LANES)
FACE = (8, NS, LANES)


def parity(axis):
    return lax.axis_index(axis) % 2


def put_faces(field, x_first, x_second, y_first, y_second, packed):
    odd_x, odd_y = parity("gx"), parity("gy")
    lane = lanes_of((NS, LANES))
    for i in range(8):
        x_first[i] = field[8 * (1 - odd_x) + i]
        x_second[i] = field[8 * odd_x + i]
    for x in range(NX):
        for i in range(2):
            y_first[2 * x + i] = field[NY * x + i + 2 * (1 - odd_y)]
            y_second[2 * x + i] = field[NY * x + i + 2 * odd_y]
    joined = pltpu.roll(field[0], (-122) % LANES, 1)
    for k in range(1, PLANES):
        joined = jnp.where(lane // 8 == k, pltpu.roll(field[k], (8 * k - 122) % LANES, 1), joined)
    packed[...] = joined


def setup(diff, pref, barrier, wt_react, factor_y, factor_zt, wt_out, diff_out, bar_out, fz_out, fy_out, fzt_pad):
    for s in range(NS):
        diff_out[s : s + 1, :] = jnp.full((1, LANES), 0.25 * diff[s], F32)
    for r in range(NR):
        bar_out[r : r + 1, :] = jnp.full((1, LANES), -barrier[r], F32)
    wt_out[...] = wt_react[...] * jnp.reshape(pref[...], (1, NR))
    fzt_pad[...] = jnp.zeros(fzt_pad.shape, F32)
    fzt_pad[:, 0:NZ] = factor_zt[...]
    cores = factor_zt.shape[0]
    wide = fz_out.shape[1]
    row = lax.broadcasted_iota(jnp.int32, (cores, wide), 0)
    lane = lanes_of((cores, wide))
    pick = (row == (lane // LANES) * NC + lane % NC).astype(F32)
    fz_out[...] = lax.dot_general(
        fzt_pad[...], pick, (((0,), (0,)), ((), ())), precision=HIGH, preferred_element_type=F32
    )
    cores = factor_y.shape[1]
    wide = fy_out.shape[1]
    row = lax.broadcasted_iota(jnp.int32, (cores, wide), 0)
    lane = lanes_of((cores, wide))
    pick = (row == (lane // LANES) * NB + (lane // NC) % NB).astype(F32)
    fy_out[...] = jnp.dot(factor_y[...], pick, precision=HIGH, preferred_element_type=F32)


def enter_kernel(state, field, *faces):
    for k in range(PLANES):
        x, y = divmod(k, NY)
        field[k] = jnp.concatenate([state[:, x, y, :], jnp.zeros((NS, LANES - NZ), F32)], axis=1)
    put_faces(field, *faces)


def source(c_state, c_now, state, field, wt, bar, stoich, base, inverse):
    inverse[...] = 1.0 / (1.5 + jnp.tanh(field[:, 0, :]))
    cells = jnp.concatenate([field[k] for k in range(PLANES)], axis=1)
    speed = lax.dot_general(wt[...], cells, (((0,), (0,)), ((), ())), precision=HIGH, preferred_element_type=F32)
    heat = jnp.concatenate(
        [jnp.exp(bar[...] * jnp.broadcast_to(inverse[k : k + 1, :], (NR, LANES))) for k in range(PLANES)], axis=1
    )
    made = jnp.dot(stoich[...], speed * heat, precision=HIGH, preferred_element_type=F32)
    for k in range(PLANES):
        value = c_now * (field[k] + made[:, k * LANES : (k + 1) * LANES])
        if state is not None:
            value = value + c_state * state[k]
        base[k] = value


def first_source_kernel(diff, pref, barrier, wt_react, factor_y, factor_zt, stoich, field, base, *refs):
    outs, (fzt_pad, inverse) = refs[:5], refs[5:]
    setup(diff, pref, barrier, wt_react, factor_y, factor_zt, *outs, fzt_pad)
    source(0.0, 1.0, None, field, outs[0], outs[2], stoich, base, inverse)


def source_kernel(rates, state, field, wt, bar, stoich, base, inverse):
    source(*rates, state, field, wt, bar, stoich, base, inverse)


def scale_of(rows):
    return jnp.exp(0.7 * jnp.log((1.5 + jnp.tanh(rows)) / 2.5))


def advance(c_now, base, field, diff, x_first, x_second, y_first, y_second, z_first, z_second, x_halo, y_halo, z_halo, full, own_k, side_k, emit):
    odd_x, odd_y, odd_z = parity("gx"), parity("gy"), parity("gz")
    for i in range(8):
        x_halo[8 * (1 - odd_x) + i] = x_first[i]
        x_halo[8 * odd_x + i] = x_second[i]
        y_halo[8 * (1 - odd_y) + i] = y_first[i]
        y_halo[8 * odd_y + i] = y_second[i]
    z_halo[1 - odd_z] = z_first[...]
    z_halo[odd_z] = z_second[...]
    lane = lanes_of((NS, LANES))
    z_ends = jnp.where(lane % 8 < 2, pltpu.roll(z_halo[1], LANES - 6, 1), pltpu.roll(z_halo[0], 2, 1))
    for k in range(PLANES):
        full[k] = jnp.where(lane < NZ, field[k], pltpu.roll(z_ends, (NZ - 8 * k) % LANES, 1))
    own_k[...] = scale_of(full[:, 0, :])
    for i in range(4):
        side_k[i : i + 1, :] = x_halo[4 + i, 0:1, :]
        side_k[4 + i : 5 + i, :] = x_halo[8 + i, 0:1, :]
        side_k[8 + i : 9 + i, :] = y_halo[2 * i + 1, 0:1, :]
        side_k[12 + i : 13 + i, :] = y_halo[8 + 2 * i, 0:1, :]
    side_k[...] = scale_of(side_k[...])
    weight = c_now * diff[...]

    def wide(row):
        return jnp.broadcast_to(row, (NS, LANES))

    def k_at(x, y):
        if x < 0:
            return wide(side_k[y : y + 1, :])
        if x >= NX:
            return wide(side_k[4 + y : 5 + y, :])
        if y < 0:
            return wide(side_k[8 + x : 9 + x, :])
        if y >= NY:
            return wide(side_k[12 + x : 13 + x, :])
        k = x * NY + y
        return wide(own_k[k : k + 1, :])

    def y_at(x, y):
        if x < 0:
            return x_halo[(x + 2) * NY + y]
        if x >= NX:
            return x_halo[8 + (x - NX) * NY + y]
        if y < 0:
            return y_halo[x * 2 + y + 2]
        if y >= NY:
            return y_halo[8 + x * 2 + y - NY]
        return full[x * NY + y]

    for k in range(PLANES):
        x, y = divmod(k, NY)
        here = full[k]
        total = k_at(x + 1, y) * (y_at(x + 2, y) - here) - k_at(x - 1, y) * (here - y_at(x - 2, y))
        total = total + (k_at(x, y + 1) * (y_at(x, y + 2) - here) - k_at(x, y - 1) * (here - y_at(x, y - 2)))
        row = own_k[k : k + 1, :]
        after = wide(pltpu.roll(row, LANES - 1, 1))
        before = wide(pltpu.roll(row, 1, 1))
        total = total + (after * (pltpu.roll(here, LANES - 2, 1) - here) - before * (here - pltpu.roll(here, 2, 1)))
        emit(k, base[k] + weight * total)


def section_kernel(c_now, *refs):
    ins, (field, *faces), scratch = refs[:9], refs[9:15], refs[15:]

    def emit(k, plane):
        field[k] = plane

    advance(c_now, *ins, *scratch, emit)
    put_faces(field, *faces)


def last_kernel(c_now, *refs):
    ins, (fz, fy), (advanced, parts), scratch = refs[:9], refs[9:11], refs[11:13], refs[13:19]
    rows = refs[19]
    lane = lanes_of((NS, LANES))

    def emit(k, plane):
        x, y = divmod(k, NY)
        advanced[:, x, y, :] = plane[:, :NZ]
        rows[k * NS : (k + 1) * NS, :] = jnp.where(lane < NZ, plane, 0.0)

    advance(c_now, *ins, *scratch, emit)
    along_z = jnp.dot(rows[...], fz[...], precision=HIGH, preferred_element_type=F32)
    n_z = fz.shape[1] // LANES
    n_y = fy.shape[1] // LANES
    for g in range(n_z):
        by_y = []
        for y in range(NY):
            value = along_z[y * NS : (y + 1) * NS, g * LANES : (g + 1) * LANES]
            for x in range(1, NX):
                k = x * NY + y
                value = jnp.where(
                    lane // 32 == x, along_z[k * NS : (k + 1) * NS, g * LANES : (g + 1) * LANES], value
                )
            by_y.append(value)
        for j in range(n_y):
            total = fy[0:1, j * LANES : (j + 1) * LANES] * by_y[0]
            for y in range(1, NY):
                total = total + fy[y : y + 1, j * LANES : (j + 1) * LANES] * by_y[y]
            parts[j * n_z + g] = total


def middle_kernel(factor_x, parts, out):
    count = parts.shape[0]
    terms = [parts[i] for i in range(count)]
    while len(terms) > 1:
        terms = [terms[i] + terms[i + 1] for i in range(0, len(terms), 2)]
    total = terms[0]
    lane = lanes_of((4, LANES))
    by_x = []
    for x in range(NX):
        value = jnp.zeros((4, LANES), F32)
        for low in range(4):
            rolled = total[4 * low : 4 * low + 4, :]
            if low != x:
                rolled = pltpu.roll(rolled, (32 * (low - x)) % LANES, 1)
            value = jnp.where(lane // 32 == low, rolled, value)
        by_x.append(value)
    for a in range(out.shape[0]):
        value = factor_x[0, a] * by_x[0]
        for x in range(1, NX):
            value = value + factor_x[x, a] * by_x[x]
        out[a] = value


def final_kernel(parts, out, rows):
    count = parts.shape[0]
    terms = [parts[i] for i in range(count)]
    while len(terms) > 1:
        terms = [terms[i] + terms[i + 1] for i in range(0, len(terms), 2)]
    total = terms[0]
    for low in range(4):
        piece = total if low == 0 else pltpu.roll(total, LANES - 32 * low, 1)
        rows[4 * low : 4 * low + 4, :] = piece
    turned = jnp.transpose(rows[...])
    for b in range(NB):
        out[0, b] = turned[b * NC : (b + 1) * NC, :]


def swapped(faces):
    x_first, x_second, y_first, y_second, packed = faces

    def swap(value, axis, start):
        pairs = []
        for i in range(start, lax.axis_size(axis) - 1, 2):
            pairs += [(i, i + 1), (i + 1, i)]
        return lax.ppermute(value, axis, pairs)

    return (
        swap(x_first, "gx", 0),
        swap(x_second, "gx", 1),
        swap(y_first, "gy", 0),
        swap(y_second, "gy", 1),
        swap(packed, "gz", 0),
        swap(packed, "gz", 1),
    )


HALO_SCRATCH = [
    pltpu.VMEM(FIELD, F32),
    pltpu.VMEM(FIELD, F32),
    pltpu.VMEM((2, NS, LANES), F32),
    pltpu.VMEM(FIELD, F32),
    pltpu.VMEM((PLANES, LANES), F32),
    pltpu.VMEM((16, LANES), F32),
]
FACES = [shaped(*FIELD), shaped(*FACE), shaped(*FACE), shaped(*FACE), shaped(*FACE), shaped(NS, LANES)]


def kernel(body, name, outs, scalars, arrays, scratch=()):
    single = not isinstance(outs, list)
    return pl.pallas_call(
        body,
        name=name,
        out_shape=outs,
        in_specs=smem(scalars) + vmem(arrays),
        out_specs=vmem(1)[0] if single else vmem(len(outs)),
        scratch_shapes=list(scratch),
        compiler_params=pltpu.CompilerParams(vmem_limit_bytes=8 * 1024 * 1024),
    )


def local(state_grid, diffusivity, prefactor_list, arrhenius_barrier, w_react, stoich_matrix, factor_x, factor_y, factor_z):
    n_x, n_y, n_z = (lax.axis_size(axis) for axis in ("gx", "gy", "gz"))
    cores_z = factor_z.shape[1]
    state, *faces = kernel(enter_kernel, "enter", FACES, 0, 1)(state_grid)
    inverse = pltpu.VMEM((PLANES, LANES), F32)
    consts = [shaped(NS, NR), shaped(NS, LANES), shaped(NR, LANES), shaped(LANES, n_z * LANES), shaped(NY, n_y * LANES)]

    halos = swapped(faces)
    base, wt, diff, bar, fz, fy = pl.pallas_call(
        first_source_kernel,
        name="first_source",
        out_shape=[shaped(*FIELD)] + consts,
        in_specs=smem(1) + vmem(1) + smem(1) + vmem(5),
        out_specs=vmem(6),
        scratch_shapes=[pltpu.VMEM((cores_z, LANES), F32), inverse],
        compiler_params=pltpu.CompilerParams(vmem_limit_bytes=8 * 1024 * 1024),
    )(diffusivity, prefactor_list, arrhenius_barrier, w_react.T, factor_y, factor_z.T, stoich_matrix, state)

    def section(c_now, base, field, halos):
        body = lambda *refs: section_kernel(c_now, *refs)
        return kernel(body, "section", FACES, 0, 9, HALO_SCRATCH)(base, field, diff, *halos)

    def base_of(c_state, c_now, field):
        body = lambda *refs: source_kernel((c_state, c_now), *refs)
        return kernel(body, "source", shaped(*FIELD), 0, 5, [inverse])(state, field, wt, bar, stoich_matrix)

    field, *faces = section(1.0, base, state, halos)
    halos = swapped(faces)
    field, *faces = section(0.25, base_of(0.75, 0.25, field), field, halos)
    halos = swapped(faces)
    base = base_of(1.0 / 3.0, 2.0 / 3.0, field)
    advanced, parts = kernel(
        lambda *refs: last_kernel(2.0 / 3.0, *refs),
        "last",
        [shaped(NS, NX, NY, NZ), shaped(n_y * n_z, NS, LANES)],
        0,
        11,
        HALO_SCRATCH + [pltpu.VMEM((PLANES * NS, LANES), F32)],
    )(base, field, diff, *halos, fz, fy)
    parts = lax.all_to_all(parts, ("gy", "gz"), 0, 0, tiled=True)
    parts = kernel(middle_kernel, "middle", shaped(n_x, 4, LANES), 1, 1)(factor_x, parts)
    parts = lax.all_to_all(parts, "gx", 0, 0, tiled=True)
    tucker_core = kernel(final_kernel, "final", shaped(1, NB, NC, NS), 0, 1, [pltpu.VMEM((NS, LANES), F32)])(parts)
    return advanced, tucker_core


def solution(mesh):
    placed = (P(None, "gx", "gy", "gz"), P(), P(), P(), P(), P(), P("gx", None), P("gy", None), P("gz", None))
    return jax.shard_map(
        local,
        mesh=mesh,
        in_specs=placed,
        out_specs=(P(None, "gx", "gy", "gz"), P("gx", "gy", "gz", None)),
        check_vma=False,
    )
```

```python
import jax
import jax.numpy as jnp
from jax import lax
from jax.experimental import pallas as pl
from jax.experimental.pallas import tpu as pltpu
from jax.sharding import PartitionSpec as P

NS, NR, NX, NY, NZ = 16, 32, 4, 4, 124
PLANES = NX * NY
LANES = 128
NB, NC = 4, 8
HIGH = lax.Precision.HIGHEST
F32 = jnp.float32


def vmem(n):
    return [pl.BlockSpec(memory_space=pltpu.VMEM)] * n


def smem(n):
    return [pl.BlockSpec(memory_space=pltpu.SMEM)] * n


def shaped(*shape):
    return jax.ShapeDtypeStruct(shape, F32)


def lanes_of(shape):
    return lax.broadcasted_iota(jnp.int32, shape, len(shape) - 1)


FIELD = (PLANES, NS, LANES)
FACE = (8, NS, LANES)


def parity(axis):
    return lax.axis_index(axis) % 2


def put_faces(field, x_first, x_second, y_first, y_second, packed):
    odd_x, odd_y = parity("gx"), parity("gy")
    lane = lanes_of((NS, LANES))
    for i in range(8):
        x_first[i] = field[8 * (1 - odd_x) + i]
        x_second[i] = field[8 * odd_x + i]
    for x in range(NX):
        for i in range(2):
            y_first[2 * x + i] = field[NY * x + i + 2 * (1 - odd_y)]
            y_second[2 * x + i] = field[NY * x + i + 2 * odd_y]
    joined = pltpu.roll(field[0], (-122) % LANES, 1)
    for k in range(1, PLANES):
        joined = jnp.where(lane // 8 == k, pltpu.roll(field[k], (8 * k - 122) % LANES, 1), joined)
    packed[...] = joined


def setup(diff, pref, barrier, wt_react, factor_y, factor_zt, wt_out, diff_out, bar_out, fz_out, fy_out, fzt_pad):
    for s in range(NS):
        diff_out[s : s + 1, :] = jnp.full((1, LANES), 0.25 * diff[s], F32)
    for r in range(NR):
        bar_out[r : r + 1, :] = jnp.full((1, LANES), -barrier[r], F32)
    wt_out[...] = wt_react[...] * jnp.reshape(pref[...], (1, NR))
    fzt_pad[...] = jnp.zeros(fzt_pad.shape, F32)
    fzt_pad[:, 0:NZ] = factor_zt[...]
    cores = factor_zt.shape[0]
    wide = fz_out.shape[1]
    row = lax.broadcasted_iota(jnp.int32, (cores, wide), 0)
    lane = lanes_of((cores, wide))
    pick = (row == (lane // LANES) * NC + lane % NC).astype(F32)
    fz_out[...] = lax.dot_general(
        fzt_pad[...], pick, (((0,), (0,)), ((), ())), precision=HIGH, preferred_element_type=F32
    )
    cores = factor_y.shape[1]
    wide = fy_out.shape[1]
    row = lax.broadcasted_iota(jnp.int32, (cores, wide), 0)
    lane = lanes_of((cores, wide))
    pick = (row == (lane // LANES) * NB + (lane // NC) % NB).astype(F32)
    fy_out[...] = jnp.dot(factor_y[...], pick, precision=HIGH, preferred_element_type=F32)


def enter_kernel(state, field, *faces):
    for k in range(PLANES):
        x, y = divmod(k, NY)
        field[k] = jnp.concatenate([state[:, x, y, :], jnp.zeros((NS, LANES - NZ), F32)], axis=1)
    put_faces(field, *faces)


def source(c_state, c_now, state, field, wt, bar, stoich, base, inverse):
    inverse[...] = 1.0 / (1.5 + jnp.tanh(field[:, 0, :]))
    cells = jnp.concatenate([field[k] for k in range(PLANES)], axis=1)
    speed = lax.dot_general(wt[...], cells, (((0,), (0,)), ((), ())), precision=HIGH, preferred_element_type=F32)
    heat = jnp.concatenate(
        [jnp.exp(bar[...] * jnp.broadcast_to(inverse[k : k + 1, :], (NR, LANES))) for k in range(PLANES)], axis=1
    )
    made = jnp.dot(stoich[...], speed * heat, precision=HIGH, preferred_element_type=F32)
    for k in range(PLANES):
        value = c_now * (field[k] + made[:, k * LANES : (k + 1) * LANES])
        if state is not None:
            value = value + c_state * state[k]
        base[k] = value


def first_source_kernel(diff, pref, barrier, wt_react, factor_y, factor_zt, stoich, field, base, *refs):
    outs, (fzt_pad, inverse) = refs[:5], refs[5:]
    setup(diff, pref, barrier, wt_react, factor_y, factor_zt, *outs, fzt_pad)
    source(0.0, 1.0, None, field, outs[0], outs[2], stoich, base, inverse)


def source_kernel(rates, state, field, wt, bar, stoich, base, inverse):
    source(*rates, state, field, wt, bar, stoich, base, inverse)


def scale_of(rows):
    return jnp.exp(0.7 * jnp.log((1.5 + jnp.tanh(rows)) / 2.5))


def advance(c_now, base, field, diff, y_second, y_first, x_first, x_second, z_first, z_second, x_halo, y_halo, z_halo, full, own_k, side_k, emit):
    odd_x, odd_y, odd_z = parity("gx"), parity("gy"), parity("gz")
    for i in range(8):
        x_halo[8 * (1 - odd_x) + i] = x_first[i]
        x_halo[8 * odd_x + i] = x_second[i]
        y_halo[8 * (1 - odd_y) + i] = y_first[i]
        y_halo[8 * odd_y + i] = y_second[i]
    z_halo[1 - odd_z] = z_first[...]
    z_halo[odd_z] = z_second[...]
    lane = lanes_of((NS, LANES))
    z_ends = jnp.where(lane % 8 < 2, pltpu.roll(z_halo[1], LANES - 6, 1), pltpu.roll(z_halo[0], 2, 1))
    for k in range(PLANES):
        full[k] = jnp.where(lane < NZ, field[k], pltpu.roll(z_ends, (NZ - 8 * k) % LANES, 1))
    own_k[...] = scale_of(full[:, 0, :])
    for i in range(4):
        side_k[i : i + 1, :] = x_halo[4 + i, 0:1, :]
        side_k[4 + i : 5 + i, :] = x_halo[8 + i, 0:1, :]
        side_k[8 + i : 9 + i, :] = y_halo[2 * i + 1, 0:1, :]
        side_k[12 + i : 13 + i, :] = y_halo[8 + 2 * i, 0:1, :]
    side_k[...] = scale_of(side_k[...])
    weight = c_now * diff[...]

    def wide(row):
        return jnp.broadcast_to(row, (NS, LANES))

    def k_at(x, y):
        if x < 0:
            return wide(side_k[y : y + 1, :])
        if x >= NX:
            return wide(side_k[4 + y : 5 + y, :])
        if y < 0:
            return wide(side_k[8 + x : 9 + x, :])
        if y >= NY:
            return wide(side_k[12 + x : 13 + x, :])
        k = x * NY + y
        return wide(own_k[k : k + 1, :])

    def y_at(x, y):
        if x < 0:
            return x_halo[(x + 2) * NY + y]
        if x >= NX:
            return x_halo[8 + (x - NX) * NY + y]
        if y < 0:
            return y_halo[x * 2 + y + 2]
        if y >= NY:
            return y_halo[8 + x * 2 + y - NY]
        return full[x * NY + y]

    for k in range(PLANES):
        x, y = divmod(k, NY)
        here = full[k]
        total = k_at(x + 1, y) * (y_at(x + 2, y) - here) - k_at(x - 1, y) * (here - y_at(x - 2, y))
        total = total + (k_at(x, y + 1) * (y_at(x, y + 2) - here) - k_at(x, y - 1) * (here - y_at(x, y - 2)))
        row = own_k[k : k + 1, :]
        after = wide(pltpu.roll(row, LANES - 1, 1))
        before = wide(pltpu.roll(row, 1, 1))
        total = total + (after * (pltpu.roll(here, LANES - 2, 1) - here) - before * (here - pltpu.roll(here, 2, 1)))
        emit(k, base[k] + weight * total)


def section_kernel(c_now, *refs):
    ins, (field, *faces), scratch = refs[:9], refs[9:15], refs[15:]

    def emit(k, plane):
        field[k] = plane

    advance(c_now, *ins, *scratch, emit)
    put_faces(field, *faces)


def last_kernel(c_now, *refs):
    ins, (fz, fy), (advanced, parts), scratch = refs[:9], refs[9:11], refs[11:13], refs[13:19]
    rows = refs[19]
    lane = lanes_of((NS, LANES))

    def emit(k, plane):
        x, y = divmod(k, NY)
        advanced[:, x, y, :] = plane[:, :NZ]
        rows[k * NS : (k + 1) * NS, :] = jnp.where(lane < NZ, plane, 0.0)

    advance(c_now, *ins, *scratch, emit)
    along_z = jnp.dot(rows[...], fz[...], precision=HIGH, preferred_element_type=F32)
    n_z = fz.shape[1] // LANES
    n_y = fy.shape[1] // LANES
    for g in range(n_z):
        by_y = []
        for y in range(NY):
            value = along_z[y * NS : (y + 1) * NS, g * LANES : (g + 1) * LANES]
            for x in range(1, NX):
                k = x * NY + y
                value = jnp.where(
                    lane // 32 == x, along_z[k * NS : (k + 1) * NS, g * LANES : (g + 1) * LANES], value
                )
            by_y.append(value)
        for j in range(n_y):
            total = fy[0:1, j * LANES : (j + 1) * LANES] * by_y[0]
            for y in range(1, NY):
                total = total + fy[y : y + 1, j * LANES : (j + 1) * LANES] * by_y[y]
            parts[j * n_z + g] = total


def middle_kernel(factor_x, parts, out):
    count = parts.shape[0]
    terms = [parts[i] for i in range(count)]
    while len(terms) > 1:
        terms = [terms[i] + terms[i + 1] for i in range(0, len(terms), 2)]
    total = terms[0]
    lane = lanes_of((4, LANES))
    by_x = []
    for x in range(NX):
        value = jnp.zeros((4, LANES), F32)
        for low in range(4):
            rolled = total[4 * low : 4 * low + 4, :]
            if low != x:
                rolled = pltpu.roll(rolled, (32 * (low - x)) % LANES, 1)
            value = jnp.where(lane // 32 == low, rolled, value)
        by_x.append(value)
    for a in range(out.shape[0]):
        value = factor_x[0, a] * by_x[0]
        for x in range(1, NX):
            value = value + factor_x[x, a] * by_x[x]
        out[a] = value


def final_kernel(parts, out, rows):
    count = parts.shape[0]
    terms = [parts[i] for i in range(count)]
    while len(terms) > 1:
        terms = [terms[i] + terms[i + 1] for i in range(0, len(terms), 2)]
    total = terms[0]
    for low in range(4):
        piece = total if low == 0 else pltpu.roll(total, LANES - 32 * low, 1)
        rows[4 * low : 4 * low + 4, :] = piece
    turned = jnp.transpose(rows[...])
    for b in range(NB):
        out[0, b] = turned[b * NC : (b + 1) * NC, :]


def swapped(faces):
    x_first, x_second, y_first, y_second, packed = faces

    def swap(value, axis, start):
        pairs = []
        for i in range(start, lax.axis_size(axis) - 1, 2):
            pairs += [(i, i + 1), (i + 1, i)]
        return lax.ppermute(value, axis, pairs)

    y_second = swap(y_second, "gy", 1)
    y_first = swap(y_first, "gy", 0)
    x_first = swap(x_first, "gx", 0)
    x_second = swap(x_second, "gx", 1)
    z_second = swap(packed, "gz", 1)
    z_first = swap(packed, "gz", 0)
    return y_second, y_first, x_first, x_second, z_first, z_second


HALO_SCRATCH = [
    pltpu.VMEM(FIELD, F32),
    pltpu.VMEM(FIELD, F32),
    pltpu.VMEM((2, NS, LANES), F32),
    pltpu.VMEM(FIELD, F32),
    pltpu.VMEM((PLANES, LANES), F32),
    pltpu.VMEM((16, LANES), F32),
]
FACES = [shaped(*FIELD), shaped(*FACE), shaped(*FACE), shaped(*FACE), shaped(*FACE), shaped(NS, LANES)]


def kernel(body, name, outs, scalars, arrays, scratch=()):
    single = not isinstance(outs, list)
    return pl.pallas_call(
        body,
        name=name,
        out_shape=outs,
        in_specs=smem(scalars) + vmem(arrays),
        out_specs=vmem(1)[0] if single else vmem(len(outs)),
        scratch_shapes=list(scratch),
        compiler_params=pltpu.CompilerParams(vmem_limit_bytes=8 * 1024 * 1024),
    )


def local(state_grid, diffusivity, prefactor_list, arrhenius_barrier, w_react, stoich_matrix, factor_x, factor_y, factor_z):
    n_x, n_y, n_z = (lax.axis_size(axis) for axis in ("gx", "gy", "gz"))
    cores_z = factor_z.shape[1]
    state, *faces = kernel(enter_kernel, "enter", FACES, 0, 1)(state_grid)
    inverse = pltpu.VMEM((PLANES, LANES), F32)
    consts = [shaped(NS, NR), shaped(NS, LANES), shaped(NR, LANES), shaped(LANES, n_z * LANES), shaped(NY, n_y * LANES)]

    halos = swapped(faces)
    base, wt, diff, bar, fz, fy = pl.pallas_call(
        first_source_kernel,
        name="first_source",
        out_shape=[shaped(*FIELD)] + consts,
        in_specs=smem(1) + vmem(1) + smem(1) + vmem(5),
        out_specs=vmem(6),
        scratch_shapes=[pltpu.VMEM((cores_z, LANES), F32), inverse],
        compiler_params=pltpu.CompilerParams(vmem_limit_bytes=8 * 1024 * 1024),
    )(diffusivity, prefactor_list, arrhenius_barrier, w_react.T, factor_y, factor_z.T, stoich_matrix, state)

    def section(c_now, base, field, halos):
        body = lambda *refs: section_kernel(c_now, *refs)
        return kernel(body, "section", FACES, 0, 9, HALO_SCRATCH)(base, field, diff, *halos)

    def base_of(c_state, c_now, field):
        body = lambda *refs: source_kernel((c_state, c_now), *refs)
        return kernel(body, "source", shaped(*FIELD), 0, 5, [inverse])(state, field, wt, bar, stoich_matrix)

    field, *faces = section(1.0, base, state, halos)
    halos = swapped(faces)
    field, *faces = section(0.25, base_of(0.75, 0.25, field), field, halos)
    halos = swapped(faces)
    base = base_of(1.0 / 3.0, 2.0 / 3.0, field)
    advanced, parts = kernel(
        lambda *refs: last_kernel(2.0 / 3.0, *refs),
        "last",
        [shaped(NS, NX, NY, NZ), shaped(n_y * n_z, NS, LANES)],
        0,
        11,
        HALO_SCRATCH + [pltpu.VMEM((PLANES * NS, LANES), F32)],
    )(base, field, diff, *halos, fz, fy)
    parts = lax.all_to_all(parts, ("gy", "gz"), 0, 0, tiled=True)
    parts = kernel(middle_kernel, "middle", shaped(n_x, 4, LANES), 1, 1)(factor_x, parts)
    parts = lax.all_to_all(parts, "gx", 0, 0, tiled=True)
    tucker_core = kernel(final_kernel, "final", shaped(1, NB, NC, NS), 0, 1, [pltpu.VMEM((NS, LANES), F32)])(parts)
    return advanced, tucker_core


def solution(mesh):
    placed = (P(None, "gx", "gy", "gz"), P(), P(), P(), P(), P(), P("gx", None), P("gy", None), P("gz", None))
    return jax.shard_map(
        local,
        mesh=mesh,
        in_specs=placed,
        out_specs=(P(None, "gx", "gy", "gz"), P("gx", "gy", "gz", None)),
        check_vma=False,
    )
```

```python
import jax
import jax.numpy as jnp
from jax import lax
from jax.experimental import pallas as pl
from jax.experimental.pallas import tpu as pltpu
from jax.sharding import PartitionSpec as P

NS, NR, NX, NY, NZ = 16, 32, 4, 4, 124
PLANES = NX * NY
LANES = 128
NB, NC = 4, 8
HIGH = lax.Precision.HIGHEST
F32 = jnp.float32


def vmem(n):
    return [pl.BlockSpec(memory_space=pltpu.VMEM)] * n


def smem(n):
    return [pl.BlockSpec(memory_space=pltpu.SMEM)] * n


def shaped(*shape):
    return jax.ShapeDtypeStruct(shape, F32)


def lanes_of(shape):
    return lax.broadcasted_iota(jnp.int32, shape, len(shape) - 1)


FIELD = (PLANES, NS, LANES)
FACE = (8, NS, LANES)


def parity(axis):
    return lax.axis_index(axis) % 2


def put_faces(field, x_first, x_second, y_first, y_second, packed):
    odd_x, odd_y = parity("gx"), parity("gy")
    lane = lanes_of((NS, LANES))
    for i in range(8):
        x_first[i] = field[8 * (1 - odd_x) + i]
        x_second[i] = field[8 * odd_x + i]
    for x in range(NX):
        for i in range(2):
            y_first[2 * x + i] = field[NY * x + i + 2 * (1 - odd_y)]
            y_second[2 * x + i] = field[NY * x + i + 2 * odd_y]
    joined = pltpu.roll(field[0], (-122) % LANES, 1)
    for k in range(1, PLANES):
        joined = jnp.where(lane // 8 == k, pltpu.roll(field[k], (8 * k - 122) % LANES, 1), joined)
    packed[...] = joined


def column(values):
    n = values.shape[0]
    row = lax.broadcasted_iota(jnp.int32, (n, n), 0)
    spread = jnp.where(row == lanes_of((n, n)), jnp.reshape(values[...], (1, n)), 0.0)
    return jnp.dot(spread, jnp.ones((n, LANES), F32), precision=HIGH, preferred_element_type=F32)


def setup(diff, pref, barrier, wt_react, stoich, factor_y, factor_zt, wt_out, stoich_out, diff_out, bar_out, fz_out, fy_out, fzt_pad):
    stoich_out[...] = stoich[...]
    diff_out[...] = 0.25 * column(diff)
    bar_out[...] = -column(barrier)
    wt_out[...] = wt_react[...] * jnp.reshape(pref[...], (1, NR))
    fzt_pad[...] = jnp.zeros(fzt_pad.shape, F32)
    fzt_pad[:, 0:NZ] = factor_zt[...]
    cores = factor_zt.shape[0]
    wide = fz_out.shape[1]
    row = lax.broadcasted_iota(jnp.int32, (cores, wide), 0)
    lane = lanes_of((cores, wide))
    pick = (row == (lane // LANES) * NC + lane % NC).astype(F32)
    fz_out[...] = lax.dot_general(
        fzt_pad[...], pick, (((0,), (0,)), ((), ())), precision=HIGH, preferred_element_type=F32
    )
    cores = factor_y.shape[1]
    wide = fy_out.shape[1]
    row = lax.broadcasted_iota(jnp.int32, (cores, wide), 0)
    lane = lanes_of((cores, wide))
    pick = (row == (lane // LANES) * NB + (lane // NC) % NB).astype(F32)
    fy_out[...] = jnp.dot(factor_y[...], pick, precision=HIGH, preferred_element_type=F32)


def enter_kernel(*refs):
    there, (field, *faces), tables, scratch = refs[:8], refs[8:14], refs[14:20], refs[20:]
    fzt_pad, here, arrived = scratch[0], scratch[1:9], scratch[9]
    copies = [pltpu.make_async_copy(there[i], here[i], arrived.at[i]) for i in range(8)]
    for copy in copies:
        copy.start()
    copies[0].wait()
    state = here[0]
    for k in range(PLANES):
        x, y = divmod(k, NY)
        field[k] = jnp.concatenate([state[:, x, y, :], jnp.zeros((NS, LANES - NZ), F32)], axis=1)
    put_faces(field, *faces)
    for copy in copies[1:]:
        copy.wait()
    setup(*here[1:], *tables, fzt_pad)


def source(c_state, c_now, state, field, wt, bar, stoich, base, inverse):
    inverse[...] = 1.0 / (1.5 + jnp.tanh(field[:, 0, :]))
    cells = jnp.concatenate([field[k] for k in range(PLANES)], axis=1)
    speed = lax.dot_general(wt[...], cells, (((0,), (0,)), ((), ())), precision=HIGH, preferred_element_type=F32)
    heat = jnp.concatenate(
        [jnp.exp(bar[...] * jnp.broadcast_to(inverse[k : k + 1, :], (NR, LANES))) for k in range(PLANES)], axis=1
    )
    made = jnp.dot(stoich[...], speed * heat, precision=HIGH, preferred_element_type=F32)
    for k in range(PLANES):
        value = c_now * (field[k] + made[:, k * LANES : (k + 1) * LANES])
        if state is not None:
            value = value + c_state * state[k]
        base[k] = value


def source_kernel(rates, *refs):
    state, *rest = refs if rates[0] else (None, *refs)
    source(*rates, state, *rest)


def scale_of(rows):
    return jnp.exp(0.7 * jnp.log((1.5 + jnp.tanh(rows)) / 2.5))


def advance(c_now, base, field, diff, y_second, y_first, x_first, x_second, z_first, z_second, x_halo, y_halo, z_halo, full, own_k, side_k, emit):
    odd_x, odd_y, odd_z = parity("gx"), parity("gy"), parity("gz")
    for i in range(8):
        x_halo[8 * (1 - odd_x) + i] = x_first[i]
        x_halo[8 * odd_x + i] = x_second[i]
        y_halo[8 * (1 - odd_y) + i] = y_first[i]
        y_halo[8 * odd_y + i] = y_second[i]
    z_halo[1 - odd_z] = z_first[...]
    z_halo[odd_z] = z_second[...]
    lane = lanes_of((NS, LANES))
    z_ends = jnp.where(lane % 8 < 2, pltpu.roll(z_halo[1], LANES - 6, 1), pltpu.roll(z_halo[0], 2, 1))
    for k in range(PLANES):
        full[k] = jnp.where(lane < NZ, field[k], pltpu.roll(z_ends, (NZ - 8 * k) % LANES, 1))
    own_k[...] = scale_of(full[:, 0, :])
    for i in range(4):
        side_k[i : i + 1, :] = x_halo[4 + i, 0:1, :]
        side_k[4 + i : 5 + i, :] = x_halo[8 + i, 0:1, :]
        side_k[8 + i : 9 + i, :] = y_halo[2 * i + 1, 0:1, :]
        side_k[12 + i : 13 + i, :] = y_halo[8 + 2 * i, 0:1, :]
    side_k[...] = scale_of(side_k[...])
    weight = c_now * diff[...]

    def wide(row):
        return jnp.broadcast_to(row, (NS, LANES))

    def k_at(x, y):
        if x < 0:
            return wide(side_k[y : y + 1, :])
        if x >= NX:
            return wide(side_k[4 + y : 5 + y, :])
        if y < 0:
            return wide(side_k[8 + x : 9 + x, :])
        if y >= NY:
            return wide(side_k[12 + x : 13 + x, :])
        k = x * NY + y
        return wide(own_k[k : k + 1, :])

    def y_at(x, y):
        if x < 0:
            return x_halo[(x + 2) * NY + y]
        if x >= NX:
            return x_halo[8 + (x - NX) * NY + y]
        if y < 0:
            return y_halo[x * 2 + y + 2]
        if y >= NY:
            return y_halo[8 + x * 2 + y - NY]
        return full[x * NY + y]

    for k in range(PLANES):
        x, y = divmod(k, NY)
        here = full[k]
        total = k_at(x + 1, y) * (y_at(x + 2, y) - here) - k_at(x - 1, y) * (here - y_at(x - 2, y))
        total = total + (k_at(x, y + 1) * (y_at(x, y + 2) - here) - k_at(x, y - 1) * (here - y_at(x, y - 2)))
        row = own_k[k : k + 1, :]
        after = wide(pltpu.roll(row, LANES - 1, 1))
        before = wide(pltpu.roll(row, 1, 1))
        total = total + (after * (pltpu.roll(here, LANES - 2, 1) - here) - before * (here - pltpu.roll(here, 2, 1)))
        emit(k, base[k] + weight * total)


def section_kernel(c_now, *refs):
    ins, (field, *faces), scratch = refs[:9], refs[9:15], refs[15:]

    def emit(k, plane):
        field[k] = plane

    advance(c_now, *ins, *scratch, emit)
    put_faces(field, *faces)


def last_kernel(c_now, *refs):
    ins, (fz, fy), (advanced, parts), scratch = refs[:9], refs[9:11], refs[11:13], refs[13:19]
    rows = refs[19]
    lane = lanes_of((NS, LANES))

    def emit(k, plane):
        x, y = divmod(k, NY)
        advanced[:, x, y, :] = plane[:, :NZ]
        rows[k * NS : (k + 1) * NS, :] = jnp.where(lane < NZ, plane, 0.0)

    advance(c_now, *ins, *scratch, emit)
    along_z = jnp.dot(rows[...], fz[...], precision=HIGH, preferred_element_type=F32)
    n_z = fz.shape[1] // LANES
    n_y = fy.shape[1] // LANES
    for g in range(n_z):
        by_y = []
        for y in range(NY):
            value = along_z[y * NS : (y + 1) * NS, g * LANES : (g + 1) * LANES]
            for x in range(1, NX):
                k = x * NY + y
                value = jnp.where(
                    lane // 32 == x, along_z[k * NS : (k + 1) * NS, g * LANES : (g + 1) * LANES], value
                )
            by_y.append(value)
        for j in range(n_y):
            total = fy[0:1, j * LANES : (j + 1) * LANES] * by_y[0]
            for y in range(1, NY):
                total = total + fy[y : y + 1, j * LANES : (j + 1) * LANES] * by_y[y]
            parts[j * n_z + g] = total


def middle_kernel(factor_x, parts, out):
    count = parts.shape[0]
    terms = [parts[i] for i in range(count)]
    while len(terms) > 1:
        terms = [terms[i] + terms[i + 1] for i in range(0, len(terms), 2)]
    total = terms[0]
    lane = lanes_of((4, LANES))
    by_x = []
    for x in range(NX):
        value = jnp.zeros((4, LANES), F32)
        for low in range(4):
            rolled = total[4 * low : 4 * low + 4, :]
            if low != x:
                rolled = pltpu.roll(rolled, (32 * (low - x)) % LANES, 1)
            value = jnp.where(lane // 32 == low, rolled, value)
        by_x.append(value)
    for a in range(out.shape[0]):
        value = factor_x[0, a] * by_x[0]
        for x in range(1, NX):
            value = value + factor_x[x, a] * by_x[x]
        out[a] = value


def final_kernel(parts, out, rows):
    count = parts.shape[0]
    terms = [parts[i] for i in range(count)]
    while len(terms) > 1:
        terms = [terms[i] + terms[i + 1] for i in range(0, len(terms), 2)]
    total = terms[0]
    for low in range(4):
        piece = total if low == 0 else pltpu.roll(total, LANES - 32 * low, 1)
        rows[4 * low : 4 * low + 4, :] = piece
    turned = jnp.transpose(rows[...])
    for b in range(NB):
        out[0, b] = turned[b * NC : (b + 1) * NC, :]


def swapped(faces):
    x_first, x_second, y_first, y_second, packed = faces

    def swap(value, axis, start):
        pairs = []
        for i in range(start, lax.axis_size(axis) - 1, 2):
            pairs += [(i, i + 1), (i + 1, i)]
        return lax.ppermute(value, axis, pairs)

    y_second = swap(y_second, "gy", 1)
    y_first = swap(y_first, "gy", 0)
    x_first = swap(x_first, "gx", 0)
    x_second = swap(x_second, "gx", 1)
    z_second = swap(packed, "gz", 1)
    z_first = swap(packed, "gz", 0)
    return y_second, y_first, x_first, x_second, z_first, z_second


HALO_SCRATCH = [
    pltpu.VMEM(FIELD, F32),
    pltpu.VMEM(FIELD, F32),
    pltpu.VMEM((2, NS, LANES), F32),
    pltpu.VMEM(FIELD, F32),
    pltpu.VMEM((PLANES, LANES), F32),
    pltpu.VMEM((16, LANES), F32),
]
FACES = [shaped(*FIELD), shaped(*FACE), shaped(*FACE), shaped(*FACE), shaped(*FACE), shaped(NS, LANES)]


def kernel(body, name, outs, scalars, arrays, scratch=()):
    single = not isinstance(outs, list)
    return pl.pallas_call(
        body,
        name=name,
        out_shape=outs,
        in_specs=smem(scalars) + vmem(arrays),
        out_specs=vmem(1)[0] if single else vmem(len(outs)),
        scratch_shapes=list(scratch),
        compiler_params=pltpu.CompilerParams(vmem_limit_bytes=8 * 1024 * 1024),
    )


def local(state_grid, diffusivity, prefactor_list, arrhenius_barrier, w_react, stoich_matrix, factor_x, factor_y, factor_z):
    n_x, n_y, n_z = (lax.axis_size(axis) for axis in ("gx", "gy", "gz"))
    inverse = pltpu.VMEM((PLANES, LANES), F32)
    tables = [shaped(NS, NR), shaped(NS, NR), shaped(NS, LANES), shaped(NR, LANES), shaped(LANES, n_z * LANES), shaped(NY, n_y * LANES)]
    ins = (state_grid, diffusivity, prefactor_list, arrhenius_barrier, w_react.T, stoich_matrix, factor_y, factor_z.T)
    entered = pl.pallas_call(
        enter_kernel,
        name="enter",
        out_shape=FACES + tables,
        in_specs=[pl.BlockSpec(memory_space=pltpu.HBM)] * len(ins),
        out_specs=vmem(12),
        scratch_shapes=[pltpu.VMEM((factor_z.shape[1], LANES), F32)]
        + [pltpu.VMEM(value.shape, F32) for value in ins]
        + [pltpu.SemaphoreType.DMA((len(ins),))],
        compiler_params=pltpu.CompilerParams(vmem_limit_bytes=8 * 1024 * 1024),
    )(*(pltpu.with_memory_space_constraint(value, pltpu.HBM) for value in ins))
    state, faces, (wt, stoich, diff, bar, fz, fy) = entered[0], entered[1:6], entered[6:]

    def section(c_now, base, field, halos):
        body = lambda *refs: section_kernel(c_now, *refs)
        return kernel(body, "section", FACES, 0, 9, HALO_SCRATCH)(base, field, diff, *halos)

    def base_of(c_state, c_now, field):
        body = lambda *refs: source_kernel((c_state, c_now), *refs)
        ins = ([state] if c_state else []) + [field, wt, bar, stoich]
        return kernel(body, "source", shaped(*FIELD), 0, len(ins), [inverse])(*ins)

    field = state
    for c_state, c_now in ((0.0, 1.0), (0.75, 0.25)):
        halos = swapped(faces)
        field, *faces = section(c_now, base_of(c_state, c_now, field), field, halos)
    halos = swapped(faces)
    base = base_of(1.0 / 3.0, 2.0 / 3.0, field)
    advanced, parts = kernel(
        lambda *refs: last_kernel(2.0 / 3.0, *refs),
        "last",
        [shaped(NS, NX, NY, NZ), shaped(n_y * n_z, NS, LANES)],
        0,
        11,
        HALO_SCRATCH + [pltpu.VMEM((PLANES * NS, LANES), F32)],
    )(base, field, diff, *halos, fz, fy)
    parts = lax.all_to_all(parts, ("gy", "gz"), 0, 0, tiled=True)
    parts = kernel(middle_kernel, "middle", shaped(n_x, 4, LANES), 1, 1)(factor_x, parts)
    parts = lax.all_to_all(parts, "gx", 0, 0, tiled=True)
    tucker_core = kernel(final_kernel, "final", shaped(1, NB, NC, NS), 0, 1, [pltpu.VMEM((NS, LANES), F32)])(parts)
    return advanced, tucker_core


def solution(mesh):
    placed = (P(None, "gx", "gy", "gz"), P(), P(), P(), P(), P(), P("gx", None), P("gy", None), P("gz", None))
    return jax.shard_map(
        local,
        mesh=mesh,
        in_specs=placed,
        out_specs=(P(None, "gx", "gy", "gz"), P("gx", "gy", "gz", None)),
        check_vma=False,
    )
```

```python
import jax
import jax.numpy as jnp
from jax import lax
from jax.experimental import pallas as pl
from jax.experimental.pallas import tpu as pltpu
from jax.sharding import PartitionSpec as P

NS, NR, NX, NY, NZ = 16, 32, 4, 4, 124
PLANES = NX * NY
LANES = 128
NB, NC = 4, 8
HIGH = lax.Precision.HIGHEST
F32 = jnp.float32


def vmem(n):
    return [pl.BlockSpec(memory_space=pltpu.VMEM)] * n


def smem(n):
    return [pl.BlockSpec(memory_space=pltpu.SMEM)] * n


def shaped(*shape):
    return jax.ShapeDtypeStruct(shape, F32)


def lanes_of(shape):
    return lax.broadcasted_iota(jnp.int32, shape, len(shape) - 1)


FIELD = (PLANES, NS, LANES)
FACE = (8, NS, LANES)


def parity(axis):
    return lax.axis_index(axis) % 2


def put_faces(field, x_first, x_second, y_first, y_second, packed):
    odd_x, odd_y = parity("gx"), parity("gy")
    lane = lanes_of((NS, LANES))
    for i in range(8):
        x_first[i] = field[8 * (1 - odd_x) + i]
        x_second[i] = field[8 * odd_x + i]
    for x in range(NX):
        for i in range(2):
            y_first[2 * x + i] = field[NY * x + i + 2 * (1 - odd_y)]
            y_second[2 * x + i] = field[NY * x + i + 2 * odd_y]
    joined = pltpu.roll(field[0], (-122) % LANES, 1)
    for k in range(1, PLANES):
        joined = jnp.where(lane // 8 == k, pltpu.roll(field[k], (8 * k - 122) % LANES, 1), joined)
    packed[...] = joined


def column(values):
    n = values.shape[0]
    row = lax.broadcasted_iota(jnp.int32, (n, n), 0)
    spread = jnp.where(row == lanes_of((n, n)), jnp.reshape(values[...], (1, n)), 0.0)
    return jnp.dot(spread, jnp.ones((n, LANES), F32), precision=HIGH, preferred_element_type=F32)


def setup(diff, pref, barrier, wt_react, stoich, factor_y, factor_zt, wt_out, stoich_out, diff_out, bar_out, fz_out, fy_out, fzt_pad):
    stoich_out[...] = stoich[...]
    diff_out[...] = 0.25 * column(diff)
    bar_out[...] = -column(barrier)
    wt_out[...] = wt_react[...] * jnp.reshape(pref[...], (1, NR))
    fzt_pad[...] = jnp.zeros(fzt_pad.shape, F32)
    fzt_pad[:, 0:NZ] = factor_zt[...]
    cores = factor_zt.shape[0]
    wide = fz_out.shape[1]
    row = lax.broadcasted_iota(jnp.int32, (cores, wide), 0)
    lane = lanes_of((cores, wide))
    pick = (row == (lane // LANES) * NC + lane % NC).astype(F32)
    fz_out[...] = lax.dot_general(
        fzt_pad[...], pick, (((0,), (0,)), ((), ())), precision=HIGH, preferred_element_type=F32
    )
    cores = factor_y.shape[1]
    wide = fy_out.shape[1]
    row = lax.broadcasted_iota(jnp.int32, (cores, wide), 0)
    lane = lanes_of((cores, wide))
    pick = (row == (lane // LANES) * NB + (lane // NC) % NB).astype(F32)
    fy_out[...] = jnp.dot(factor_y[...], pick, precision=HIGH, preferred_element_type=F32)


def enter_kernel(*refs):
    there, (field, *faces), tables, scratch = refs[:8], refs[8:14], refs[14:20], refs[20:]
    fzt_pad, here, arrived = scratch[0], scratch[1:9], scratch[9]
    copies = [pltpu.make_async_copy(there[i], here[i], arrived.at[i]) for i in range(8)]
    for copy in copies:
        copy.start()
    copies[0].wait()
    state = here[0]
    for k in range(PLANES):
        x, y = divmod(k, NY)
        field[k] = jnp.concatenate([state[:, x, y, :], jnp.zeros((NS, LANES - NZ), F32)], axis=1)
    put_faces(field, *faces)
    for copy in copies[1:]:
        copy.wait()
    setup(*here[1:], *tables, fzt_pad)


def source(c_state, c_now, state, field, wt, bar, stoich, base, inverse):
    inverse[...] = 1.0 / (1.5 + jnp.tanh(field[:, 0, :]))
    cells = jnp.concatenate([field[k] for k in range(PLANES)], axis=1)
    speed = lax.dot_general(wt[...], cells, (((0,), (0,)), ((), ())), precision=HIGH, preferred_element_type=F32)
    heat = jnp.concatenate(
        [jnp.exp(bar[...] * jnp.broadcast_to(inverse[k : k + 1, :], (NR, LANES))) for k in range(PLANES)], axis=1
    )
    made = jnp.dot(stoich[...], speed * heat, precision=HIGH, preferred_element_type=F32)
    for k in range(PLANES):
        value = c_now * (field[k] + made[:, k * LANES : (k + 1) * LANES])
        if state is not None:
            value = value + c_state * state[k]
        base[k] = value


def source_kernel(rates, *refs):
    state, *rest = refs if rates[0] else (None, *refs)
    source(*rates, state, *rest)


def scale_of(rows):
    return jnp.exp(0.7 * jnp.log((1.5 + jnp.tanh(rows)) / 2.5))


def advance(c_now, base, field, diff, x_first, x_second, y_second, y_first, z_first, z_second, x_halo, y_halo, z_halo, full, own_k, side_k, emit):
    odd_x, odd_y, odd_z = parity("gx"), parity("gy"), parity("gz")
    for i in range(8):
        x_halo[8 * (1 - odd_x) + i] = x_first[i]
        x_halo[8 * odd_x + i] = x_second[i]
        y_halo[8 * (1 - odd_y) + i] = y_first[i]
        y_halo[8 * odd_y + i] = y_second[i]
    z_halo[1 - odd_z] = z_first[...]
    z_halo[odd_z] = z_second[...]
    lane = lanes_of((NS, LANES))
    z_ends = jnp.where(lane % 8 < 2, pltpu.roll(z_halo[1], LANES - 6, 1), pltpu.roll(z_halo[0], 2, 1))
    for k in range(PLANES):
        full[k] = jnp.where(lane < NZ, field[k], pltpu.roll(z_ends, (NZ - 8 * k) % LANES, 1))
    own_k[...] = scale_of(full[:, 0, :])
    for i in range(4):
        side_k[i : i + 1, :] = x_halo[4 + i, 0:1, :]
        side_k[4 + i : 5 + i, :] = x_halo[8 + i, 0:1, :]
        side_k[8 + i : 9 + i, :] = y_halo[2 * i + 1, 0:1, :]
        side_k[12 + i : 13 + i, :] = y_halo[8 + 2 * i, 0:1, :]
    side_k[...] = scale_of(side_k[...])
    weight = c_now * diff[...]

    def wide(row):
        return jnp.broadcast_to(row, (NS, LANES))

    def k_at(x, y):
        if x < 0:
            return wide(side_k[y : y + 1, :])
        if x >= NX:
            return wide(side_k[4 + y : 5 + y, :])
        if y < 0:
            return wide(side_k[8 + x : 9 + x, :])
        if y >= NY:
            return wide(side_k[12 + x : 13 + x, :])
        k = x * NY + y
        return wide(own_k[k : k + 1, :])

    def y_at(x, y):
        if x < 0:
            return x_halo[(x + 2) * NY + y]
        if x >= NX:
            return x_halo[8 + (x - NX) * NY + y]
        if y < 0:
            return y_halo[x * 2 + y + 2]
        if y >= NY:
            return y_halo[8 + x * 2 + y - NY]
        return full[x * NY + y]

    for k in range(PLANES):
        x, y = divmod(k, NY)
        here = full[k]
        total = k_at(x + 1, y) * (y_at(x + 2, y) - here) - k_at(x - 1, y) * (here - y_at(x - 2, y))
        total = total + (k_at(x, y + 1) * (y_at(x, y + 2) - here) - k_at(x, y - 1) * (here - y_at(x, y - 2)))
        row = own_k[k : k + 1, :]
        after = wide(pltpu.roll(row, LANES - 1, 1))
        before = wide(pltpu.roll(row, 1, 1))
        total = total + (after * (pltpu.roll(here, LANES - 2, 1) - here) - before * (here - pltpu.roll(here, 2, 1)))
        emit(k, base[k] + weight * total)


def section_kernel(c_now, *refs):
    ins, (field, *faces), scratch = refs[:9], refs[9:15], refs[15:]

    def emit(k, plane):
        field[k] = plane

    advance(c_now, *ins, *scratch, emit)
    put_faces(field, *faces)


def last_kernel(c_now, *refs):
    ins, (fz, fy), (advanced, parts), scratch = refs[:9], refs[9:11], refs[11:13], refs[13:19]
    rows = refs[19]
    lane = lanes_of((NS, LANES))

    def emit(k, plane):
        x, y = divmod(k, NY)
        advanced[:, x, y, :] = plane[:, :NZ]
        rows[k * NS : (k + 1) * NS, :] = jnp.where(lane < NZ, plane, 0.0)

    advance(c_now, *ins, *scratch, emit)
    along_z = jnp.dot(rows[...], fz[...], precision=HIGH, preferred_element_type=F32)
    n_z = fz.shape[1] // LANES
    n_y = fy.shape[1] // LANES
    for g in range(n_z):
        by_y = []
        for y in range(NY):
            value = along_z[y * NS : (y + 1) * NS, g * LANES : (g + 1) * LANES]
            for x in range(1, NX):
                k = x * NY + y
                value = jnp.where(
                    lane // 32 == x, along_z[k * NS : (k + 1) * NS, g * LANES : (g + 1) * LANES], value
                )
            by_y.append(value)
        for j in range(n_y):
            total = fy[0:1, j * LANES : (j + 1) * LANES] * by_y[0]
            for y in range(1, NY):
                total = total + fy[y : y + 1, j * LANES : (j + 1) * LANES] * by_y[y]
            parts[j * n_z + g] = total


def middle_kernel(factor_x, parts, out):
    count = parts.shape[0]
    terms = [parts[i] for i in range(count)]
    while len(terms) > 1:
        terms = [terms[i] + terms[i + 1] for i in range(0, len(terms), 2)]
    total = terms[0]
    lane = lanes_of((4, LANES))
    by_x = []
    for x in range(NX):
        value = jnp.zeros((4, LANES), F32)
        for low in range(4):
            rolled = total[4 * low : 4 * low + 4, :]
            if low != x:
                rolled = pltpu.roll(rolled, (32 * (low - x)) % LANES, 1)
            value = jnp.where(lane // 32 == low, rolled, value)
        by_x.append(value)
    for a in range(out.shape[0]):
        value = factor_x[0, a] * by_x[0]
        for x in range(1, NX):
            value = value + factor_x[x, a] * by_x[x]
        out[a] = value


def final_kernel(parts, out, rows):
    count = parts.shape[0]
    terms = [parts[i] for i in range(count)]
    while len(terms) > 1:
        terms = [terms[i] + terms[i + 1] for i in range(0, len(terms), 2)]
    total = terms[0]
    for low in range(4):
        piece = total if low == 0 else pltpu.roll(total, LANES - 32 * low, 1)
        rows[4 * low : 4 * low + 4, :] = piece
    turned = jnp.transpose(rows[...])
    for b in range(NB):
        out[0, b] = turned[b * NC : (b + 1) * NC, :]


def swapped(faces):
    x_first, x_second, y_first, y_second, packed = faces

    def swap(value, axis, start):
        pairs = []
        for i in range(start, lax.axis_size(axis) - 1, 2):
            pairs += [(i, i + 1), (i + 1, i)]
        return lax.ppermute(value, axis, pairs)

    y_second = swap(y_second, "gy", 1)
    y_first = swap(y_first, "gy", 0)
    x_first = swap(x_first, "gx", 0)
    x_second = swap(x_second, "gx", 1)
    z_second = swap(packed, "gz", 1)
    z_first = swap(packed, "gz", 0)
    return x_first, x_second, y_second, y_first, z_first, z_second


HALO_SCRATCH = [
    pltpu.VMEM(FIELD, F32),
    pltpu.VMEM(FIELD, F32),
    pltpu.VMEM((2, NS, LANES), F32),
    pltpu.VMEM(FIELD, F32),
    pltpu.VMEM((PLANES, LANES), F32),
    pltpu.VMEM((16, LANES), F32),
]
FACES = [shaped(*FIELD), shaped(*FACE), shaped(*FACE), shaped(*FACE), shaped(*FACE), shaped(NS, LANES)]


def kernel(body, name, outs, scalars, arrays, scratch=()):
    single = not isinstance(outs, list)
    return pl.pallas_call(
        body,
        name=name,
        out_shape=outs,
        in_specs=smem(scalars) + vmem(arrays),
        out_specs=vmem(1)[0] if single else vmem(len(outs)),
        scratch_shapes=list(scratch),
        compiler_params=pltpu.CompilerParams(vmem_limit_bytes=8 * 1024 * 1024),
    )


def local(state_grid, diffusivity, prefactor_list, arrhenius_barrier, w_react, stoich_matrix, factor_x, factor_y, factor_z):
    n_x, n_y, n_z = (lax.axis_size(axis) for axis in ("gx", "gy", "gz"))
    inverse = pltpu.VMEM((PLANES, LANES), F32)
    tables = [shaped(NS, NR), shaped(NS, NR), shaped(NS, LANES), shaped(NR, LANES), shaped(LANES, n_z * LANES), shaped(NY, n_y * LANES)]
    ins = (state_grid, diffusivity, prefactor_list, arrhenius_barrier, w_react.T, stoich_matrix, factor_y, factor_z.T)
    entered = pl.pallas_call(
        enter_kernel,
        name="enter",
        out_shape=FACES + tables,
        in_specs=[pl.BlockSpec(memory_space=pltpu.HBM)] * len(ins),
        out_specs=vmem(12),
        scratch_shapes=[pltpu.VMEM((factor_z.shape[1], LANES), F32)]
        + [pltpu.VMEM(value.shape, F32) for value in ins]
        + [pltpu.SemaphoreType.DMA((len(ins),))],
        compiler_params=pltpu.CompilerParams(vmem_limit_bytes=8 * 1024 * 1024),
    )(*(pltpu.with_memory_space_constraint(value, pltpu.HBM) for value in ins))
    state, faces, (wt, stoich, diff, bar, fz, fy) = entered[0], entered[1:6], entered[6:]

    def section(c_now, base, field, halos):
        body = lambda *refs: section_kernel(c_now, *refs)
        return kernel(body, "section", FACES, 0, 9, HALO_SCRATCH)(base, field, diff, *halos)

    def base_of(c_state, c_now, field):
        body = lambda *refs: source_kernel((c_state, c_now), *refs)
        ins = ([state] if c_state else []) + [field, wt, bar, stoich]
        return kernel(body, "source", shaped(*FIELD), 0, len(ins), [inverse])(*ins)

    field = state
    for c_state, c_now in ((0.0, 1.0), (0.75, 0.25)):
        halos = swapped(faces)
        field, *faces = section(c_now, base_of(c_state, c_now, field), field, halos)
    halos = swapped(faces)
    base = base_of(1.0 / 3.0, 2.0 / 3.0, field)
    advanced, parts = kernel(
        lambda *refs: last_kernel(2.0 / 3.0, *refs),
        "last",
        [shaped(NS, NX, NY, NZ), shaped(n_y * n_z, NS, LANES)],
        0,
        11,
        HALO_SCRATCH + [pltpu.VMEM((PLANES * NS, LANES), F32)],
    )(base, field, diff, *halos, fz, fy)
    parts = lax.all_to_all(parts, ("gy", "gz"), 0, 0, tiled=True)
    parts = kernel(middle_kernel, "middle", shaped(n_x, 4, LANES), 1, 1)(factor_x, parts)
    parts = lax.all_to_all(parts, "gx", 0, 0, tiled=True)
    tucker_core = kernel(final_kernel, "final", shaped(1, NB, NC, NS), 0, 1, [pltpu.VMEM((NS, LANES), F32)])(parts)
    return advanced, tucker_core


def solution(mesh):
    placed = (P(None, "gx", "gy", "gz"), P(), P(), P(), P(), P(), P("gx", None), P("gy", None), P("gz", None))
    return jax.shard_map(
        local,
        mesh=mesh,
        in_specs=placed,
        out_specs=(P(None, "gx", "gy", "gz"), P("gx", "gy", "gz", None)),
        check_vma=False,
    )
```

```python
import jax
import jax.numpy as jnp
from jax import lax
from jax.experimental import pallas as pl
from jax.experimental.pallas import tpu as pltpu
from jax.sharding import PartitionSpec as P

NS, NR, NX, NY, NZ = 16, 32, 4, 4, 124
PLANES = NX * NY
LANES = 128
NB, NC = 4, 8
HIGH = lax.Precision.HIGHEST
F32 = jnp.float32


def vmem(n):
    return [pl.BlockSpec(memory_space=pltpu.VMEM)] * n


def smem(n):
    return [pl.BlockSpec(memory_space=pltpu.SMEM)] * n


def shaped(*shape):
    return jax.ShapeDtypeStruct(shape, F32)


def lanes_of(shape):
    return lax.broadcasted_iota(jnp.int32, shape, len(shape) - 1)


FIELD = (PLANES, NS, LANES)
FACE = (8, NS, LANES)


def parity(axis):
    return lax.axis_index(axis) % 2


def put_faces(field, x_first, x_second, y_first, y_second, packed):
    odd_x, odd_y = parity("gx"), parity("gy")
    lane = lanes_of((NS, LANES))
    for i in range(8):
        x_first[i] = field[8 * (1 - odd_x) + i]
        x_second[i] = field[8 * odd_x + i]
    for x in range(NX):
        for i in range(2):
            y_first[2 * x + i] = field[NY * x + i + 2 * (1 - odd_y)]
            y_second[2 * x + i] = field[NY * x + i + 2 * odd_y]
    joined = pltpu.roll(field[0], (-122) % LANES, 1)
    for k in range(1, PLANES):
        joined = jnp.where(lane // 8 == k, pltpu.roll(field[k], (8 * k - 122) % LANES, 1), joined)
    packed[...] = joined


def column(values):
    n = values.shape[0]
    row = lax.broadcasted_iota(jnp.int32, (n, n), 0)
    spread = jnp.where(row == lanes_of((n, n)), jnp.reshape(values[...], (1, n)), 0.0)
    return jnp.dot(spread, jnp.ones((n, LANES), F32), precision=HIGH, preferred_element_type=F32)


def setup(diff, pref, barrier, wt_react, stoich, factor_y, factor_zt, wt_out, stoich_out, diff_out, bar_out, fz_out, fy_out, fzt_pad):
    stoich_out[...] = stoich[...]
    diff_out[...] = 0.25 * column(diff)
    bar_out[...] = -column(barrier)
    wt_out[...] = wt_react[...] * jnp.reshape(pref[...], (1, NR))
    fzt_pad[...] = jnp.zeros(fzt_pad.shape, F32)
    fzt_pad[:, 0:NZ] = factor_zt[...]
    cores = factor_zt.shape[0]
    wide = fz_out.shape[1]
    row = lax.broadcasted_iota(jnp.int32, (cores, wide), 0)
    lane = lanes_of((cores, wide))
    pick = (row == (lane // LANES) * NC + lane % NC).astype(F32)
    fz_out[...] = lax.dot_general(
        fzt_pad[...], pick, (((0,), (0,)), ((), ())), precision=HIGH, preferred_element_type=F32
    )
    cores = factor_y.shape[1]
    wide = fy_out.shape[1]
    row = lax.broadcasted_iota(jnp.int32, (cores, wide), 0)
    lane = lanes_of((cores, wide))
    pick = (row == (lane // LANES) * NB + (lane // NC) % NB).astype(F32)
    fy_out[...] = jnp.dot(factor_y[...], pick, precision=HIGH, preferred_element_type=F32)


def enter_kernel(*refs):
    there, (field, *faces), tables, scratch = refs[:8], refs[8:14], refs[14:20], refs[20:]
    fzt_pad, here, arrived = scratch[0], scratch[1:9], scratch[9]
    copies = [pltpu.make_async_copy(there[i], here[i], arrived.at[i]) for i in range(8)]
    for copy in copies:
        copy.start()
    copies[0].wait()
    state = here[0]
    for k in range(PLANES):
        x, y = divmod(k, NY)
        field[k] = jnp.concatenate([state[:, x, y, :], jnp.zeros((NS, LANES - NZ), F32)], axis=1)
    put_faces(field, *faces)
    for copy in copies[1:]:
        copy.wait()
    setup(*here[1:], *tables, fzt_pad)


def source(c_state, c_now, state, field, wt, bar, stoich, base, inverse):
    inverse[...] = 1.0 / (1.5 + jnp.tanh(field[:, 0, :]))
    cells = jnp.concatenate([field[k] for k in range(PLANES)], axis=1)
    speed = lax.dot_general(wt[...], cells, (((0,), (0,)), ((), ())), precision=HIGH, preferred_element_type=F32)
    heat = jnp.concatenate(
        [jnp.exp(bar[...] * jnp.broadcast_to(inverse[k : k + 1, :], (NR, LANES))) for k in range(PLANES)], axis=1
    )
    made = jnp.dot(stoich[...], speed * heat, precision=HIGH, preferred_element_type=F32)
    for k in range(PLANES):
        value = c_now * (field[k] + made[:, k * LANES : (k + 1) * LANES])
        if state is not None:
            value = value + c_state * state[k]
        base[k] = value


def source_kernel(rates, *refs):
    state, *rest = refs if rates[0] else (None, *refs)
    source(*rates, state, *rest)


def scale_of(rows):
    return jnp.exp(0.7 * jnp.log((1.5 + jnp.tanh(rows)) / 2.5))


def advance(c_now, base, field, diff, x_first, x_second, y_first, y_second, z_first, z_second, x_halo, y_halo, z_halo, full, own_k, side_k, emit):
    odd_x, odd_y, odd_z = parity("gx"), parity("gy"), parity("gz")
    for i in range(8):
        x_halo[8 * (1 - odd_x) + i] = x_first[i]
        x_halo[8 * odd_x + i] = x_second[i]
        y_halo[8 * (1 - odd_y) + i] = y_first[i]
        y_halo[8 * odd_y + i] = y_second[i]
    z_halo[1 - odd_z] = z_first[...]
    z_halo[odd_z] = z_second[...]
    lane = lanes_of((NS, LANES))
    z_ends = jnp.where(lane % 8 < 2, pltpu.roll(z_halo[1], LANES - 6, 1), pltpu.roll(z_halo[0], 2, 1))
    for k in range(PLANES):
        full[k] = jnp.where(lane < NZ, field[k], pltpu.roll(z_ends, (NZ - 8 * k) % LANES, 1))
    own_k[...] = scale_of(full[:, 0, :])
    for i in range(4):
        side_k[i : i + 1, :] = x_halo[4 + i, 0:1, :]
        side_k[4 + i : 5 + i, :] = x_halo[8 + i, 0:1, :]
        side_k[8 + i : 9 + i, :] = y_halo[2 * i + 1, 0:1, :]
        side_k[12 + i : 13 + i, :] = y_halo[8 + 2 * i, 0:1, :]
    side_k[...] = scale_of(side_k[...])
    weight = c_now * diff[...]

    def wide(row):
        return jnp.broadcast_to(row, (NS, LANES))

    def k_at(x, y):
        if x < 0:
            return wide(side_k[y : y + 1, :])
        if x >= NX:
            return wide(side_k[4 + y : 5 + y, :])
        if y < 0:
            return wide(side_k[8 + x : 9 + x, :])
        if y >= NY:
            return wide(side_k[12 + x : 13 + x, :])
        k = x * NY + y
        return wide(own_k[k : k + 1, :])

    def y_at(x, y):
        if x < 0:
            return x_halo[(x + 2) * NY + y]
        if x >= NX:
            return x_halo[8 + (x - NX) * NY + y]
        if y < 0:
            return y_halo[x * 2 + y + 2]
        if y >= NY:
            return y_halo[8 + x * 2 + y - NY]
        return full[x * NY + y]

    for k in range(PLANES):
        x, y = divmod(k, NY)
        here = full[k]
        total = k_at(x + 1, y) * (y_at(x + 2, y) - here) - k_at(x - 1, y) * (here - y_at(x - 2, y))
        total = total + (k_at(x, y + 1) * (y_at(x, y + 2) - here) - k_at(x, y - 1) * (here - y_at(x, y - 2)))
        row = own_k[k : k + 1, :]
        after = wide(pltpu.roll(row, LANES - 1, 1))
        before = wide(pltpu.roll(row, 1, 1))
        total = total + (after * (pltpu.roll(here, LANES - 2, 1) - here) - before * (here - pltpu.roll(here, 2, 1)))
        emit(k, base[k] + weight * total)


def section_kernel(c_now, *refs):
    ins, (field, *faces), scratch = refs[:9], refs[9:15], refs[15:]

    def emit(k, plane):
        field[k] = plane

    advance(c_now, *ins, *scratch, emit)
    put_faces(field, *faces)


def last_kernel(c_now, *refs):
    ins, (fz, fy), (advanced, parts), scratch = refs[:9], refs[9:11], refs[11:13], refs[13:19]
    rows = refs[19]
    lane = lanes_of((NS, LANES))

    def emit(k, plane):
        x, y = divmod(k, NY)
        advanced[:, x, y, :] = plane[:, :NZ]
        rows[k * NS : (k + 1) * NS, :] = jnp.where(lane < NZ, plane, 0.0)

    advance(c_now, *ins, *scratch, emit)
    along_z = jnp.dot(rows[...], fz[...], precision=HIGH, preferred_element_type=F32)
    n_z = fz.shape[1] // LANES
    n_y = fy.shape[1] // LANES
    for g in range(n_z):
        by_y = []
        for y in range(NY):
            value = along_z[y * NS : (y + 1) * NS, g * LANES : (g + 1) * LANES]
            for x in range(1, NX):
                k = x * NY + y
                value = jnp.where(
                    lane // 32 == x, along_z[k * NS : (k + 1) * NS, g * LANES : (g + 1) * LANES], value
                )
            by_y.append(value)
        for j in range(n_y):
            total = fy[0:1, j * LANES : (j + 1) * LANES] * by_y[0]
            for y in range(1, NY):
                total = total + fy[y : y + 1, j * LANES : (j + 1) * LANES] * by_y[y]
            parts[j * n_z + g] = total


def middle_kernel(factor_x, parts, out):
    count = parts.shape[0]
    terms = [parts[i] for i in range(count)]
    while len(terms) > 1:
        terms = [terms[i] + terms[i + 1] for i in range(0, len(terms), 2)]
    total = terms[0]
    lane = lanes_of((4, LANES))
    by_x = []
    for x in range(NX):
        value = jnp.zeros((4, LANES), F32)
        for low in range(4):
            rolled = total[4 * low : 4 * low + 4, :]
            if low != x:
                rolled = pltpu.roll(rolled, (32 * (low - x)) % LANES, 1)
            value = jnp.where(lane // 32 == low, rolled, value)
        by_x.append(value)
    for a in range(out.shape[0]):
        value = factor_x[0, a] * by_x[0]
        for x in range(1, NX):
            value = value + factor_x[x, a] * by_x[x]
        out[a] = value


def final_kernel(parts, out, rows):
    count = parts.shape[0]
    terms = [parts[i] for i in range(count)]
    while len(terms) > 1:
        terms = [terms[i] + terms[i + 1] for i in range(0, len(terms), 2)]
    total = terms[0]
    for low in range(4):
        piece = total if low == 0 else pltpu.roll(total, LANES - 32 * low, 1)
        rows[4 * low : 4 * low + 4, :] = piece
    turned = jnp.transpose(rows[...])
    for b in range(NB):
        out[0, b] = turned[b * NC : (b + 1) * NC, :]


def swapped(faces):
    x_first, x_second, y_first, y_second, packed = faces

    def swap(value, axis, start):
        pairs = []
        for i in range(start, lax.axis_size(axis) - 1, 2):
            pairs += [(i, i + 1), (i + 1, i)]
        return lax.ppermute(value, axis, pairs)

    y_second = swap(y_second, "gy", 1)
    y_first = swap(y_first, "gy", 0)
    x_first = swap(x_first, "gx", 0)
    x_second = swap(x_second, "gx", 1)
    z_second = swap(packed, "gz", 1)
    z_first = swap(packed, "gz", 0)
    return x_first, x_second, y_first, y_second, z_first, z_second


HALO_SCRATCH = [
    pltpu.VMEM(FIELD, F32),
    pltpu.VMEM(FIELD, F32),
    pltpu.VMEM((2, NS, LANES), F32),
    pltpu.VMEM(FIELD, F32),
    pltpu.VMEM((PLANES, LANES), F32),
    pltpu.VMEM((16, LANES), F32),
]
FACES = [shaped(*FIELD), shaped(*FACE), shaped(*FACE), shaped(*FACE), shaped(*FACE), shaped(NS, LANES)]


def kernel(body, name, outs, scalars, arrays, scratch=()):
    single = not isinstance(outs, list)
    return pl.pallas_call(
        body,
        name=name,
        out_shape=outs,
        in_specs=smem(scalars) + vmem(arrays),
        out_specs=vmem(1)[0] if single else vmem(len(outs)),
        scratch_shapes=list(scratch),
        compiler_params=pltpu.CompilerParams(vmem_limit_bytes=8 * 1024 * 1024),
    )


def local(state_grid, diffusivity, prefactor_list, arrhenius_barrier, w_react, stoich_matrix, factor_x, factor_y, factor_z):
    n_x, n_y, n_z = (lax.axis_size(axis) for axis in ("gx", "gy", "gz"))
    inverse = pltpu.VMEM((PLANES, LANES), F32)
    tables = [shaped(NS, NR), shaped(NS, NR), shaped(NS, LANES), shaped(NR, LANES), shaped(LANES, n_z * LANES), shaped(NY, n_y * LANES)]
    ins = (state_grid, diffusivity, prefactor_list, arrhenius_barrier, w_react.T, stoich_matrix, factor_y, factor_z.T)
    entered = pl.pallas_call(
        enter_kernel,
        name="enter",
        out_shape=FACES + tables,
        in_specs=[pl.BlockSpec(memory_space=pltpu.HBM)] * len(ins),
        out_specs=vmem(12),
        scratch_shapes=[pltpu.VMEM((factor_z.shape[1], LANES), F32)]
        + [pltpu.VMEM(value.shape, F32) for value in ins]
        + [pltpu.SemaphoreType.DMA((len(ins),))],
        compiler_params=pltpu.CompilerParams(vmem_limit_bytes=8 * 1024 * 1024),
    )(*(pltpu.with_memory_space_constraint(value, pltpu.HBM) for value in ins))
    state, faces, (wt, stoich, diff, bar, fz, fy) = entered[0], entered[1:6], entered[6:]

    def section(c_now, base, field, halos):
        body = lambda *refs: section_kernel(c_now, *refs)
        return kernel(body, "section", FACES, 0, 9, HALO_SCRATCH)(base, field, diff, *halos)

    def base_of(c_state, c_now, field):
        body = lambda *refs: source_kernel((c_state, c_now), *refs)
        ins = ([state] if c_state else []) + [field, wt, bar, stoich]
        return kernel(body, "source", shaped(*FIELD), 0, len(ins), [inverse])(*ins)

    field = state
    for c_state, c_now in ((0.0, 1.0), (0.75, 0.25)):
        halos = swapped(faces)
        field, *faces = section(c_now, base_of(c_state, c_now, field), field, halos)
    halos = swapped(faces)
    base = base_of(1.0 / 3.0, 2.0 / 3.0, field)
    advanced, parts = kernel(
        lambda *refs: last_kernel(2.0 / 3.0, *refs),
        "last",
        [shaped(NS, NX, NY, NZ), shaped(n_y * n_z, NS, LANES)],
        0,
        11,
        HALO_SCRATCH + [pltpu.VMEM((PLANES * NS, LANES), F32)],
    )(base, field, diff, *halos, fz, fy)
    parts = lax.all_to_all(parts, ("gy", "gz"), 0, 0, tiled=True)
    parts = kernel(middle_kernel, "middle", shaped(n_x, 4, LANES), 1, 1)(factor_x, parts)
    parts = lax.all_to_all(parts, "gx", 0, 0, tiled=True)
    tucker_core = kernel(final_kernel, "final", shaped(1, NB, NC, NS), 0, 1, [pltpu.VMEM((NS, LANES), F32)])(parts)
    return advanced, tucker_core


def solution(mesh):
    placed = (P(None, "gx", "gy", "gz"), P(), P(), P(), P(), P(), P("gx", None), P("gy", None), P("gz", None))
    return jax.shard_map(
        local,
        mesh=mesh,
        in_specs=placed,
        out_specs=(P(None, "gx", "gy", "gz"), P("gx", "gy", "gz", None)),
        check_vma=False,
    )
```

```python
import jax
import jax.numpy as jnp
from jax import lax
from jax.experimental import pallas as pl
from jax.experimental.pallas import tpu as pltpu
from jax.sharding import PartitionSpec as P

NS, NR, NX, NY, NZ = 16, 32, 4, 4, 124
PLANES = NX * NY
LANES = 128
NB, NC = 4, 8
HIGH = lax.Precision.HIGHEST
F32 = jnp.float32


def vmem(n):
    return [pl.BlockSpec(memory_space=pltpu.VMEM)] * n


def smem(n):
    return [pl.BlockSpec(memory_space=pltpu.SMEM)] * n


def shaped(*shape):
    return jax.ShapeDtypeStruct(shape, F32)


def lanes_of(shape):
    return lax.broadcasted_iota(jnp.int32, shape, len(shape) - 1)


FIELD = (PLANES, NS, LANES)
FACE = (8, NS, LANES)


def parity(axis):
    return lax.axis_index(axis) % 2


def put_faces(field, x_first, x_second, y_first, y_second, packed):
    odd_x, odd_y = parity("gx"), parity("gy")
    lane = lanes_of((NS, LANES))
    for i in range(8):
        x_first[i] = field[8 * (1 - odd_x) + i]
        x_second[i] = field[8 * odd_x + i]
    for x in range(NX):
        for i in range(2):
            y_first[2 * x + i] = field[NY * x + i + 2 * (1 - odd_y)]
            y_second[2 * x + i] = field[NY * x + i + 2 * odd_y]
    joined = pltpu.roll(field[0], (-122) % LANES, 1)
    for k in range(1, PLANES):
        joined = jnp.where(lane // 8 == k, pltpu.roll(field[k], (8 * k - 122) % LANES, 1), joined)
    packed[...] = joined


def column(values):
    n = values.shape[0]
    row = lax.broadcasted_iota(jnp.int32, (n, n), 0)
    spread = jnp.where(row == lanes_of((n, n)), jnp.reshape(values[...], (1, n)), 0.0)
    return jnp.dot(spread, jnp.ones((n, LANES), F32), precision=HIGH, preferred_element_type=F32)


def setup(diff, pref, barrier, wt_react, stoich, factor_y, factor_zt, wt_out, stoich_out, diff_out, bar_out, fz_out, fy_out, fzt_pad):
    stoich_out[...] = stoich[...]
    diff_out[...] = 0.25 * column(diff)
    bar_out[...] = -column(barrier)
    wt_out[...] = wt_react[...] * jnp.reshape(pref[...], (1, NR))
    fzt_pad[...] = jnp.zeros(fzt_pad.shape, F32)
    fzt_pad[:, 0:NZ] = factor_zt[...]
    cores = factor_zt.shape[0]
    wide = fz_out.shape[1]
    row = lax.broadcasted_iota(jnp.int32, (cores, wide), 0)
    lane = lanes_of((cores, wide))
    pick = (row == (lane // LANES) * NC + lane % NC).astype(F32)
    fz_out[...] = lax.dot_general(
        fzt_pad[...], pick, (((0,), (0,)), ((), ())), precision=HIGH, preferred_element_type=F32
    )
    cores = factor_y.shape[1]
    wide = fy_out.shape[1]
    row = lax.broadcasted_iota(jnp.int32, (cores, wide), 0)
    lane = lanes_of((cores, wide))
    pick = (row == (lane // LANES) * NB + (lane // NC) % NB).astype(F32)
    fy_out[...] = jnp.dot(factor_y[...], pick, precision=HIGH, preferred_element_type=F32)


def enter_kernel(*refs):
    there, (field, *faces), tables, scratch = refs[:8], refs[8:14], refs[14:20], refs[20:]
    fzt_pad, here, arrived = scratch[0], scratch[1:9], scratch[9]
    copies = [pltpu.make_async_copy(there[i], here[i], arrived.at[i]) for i in range(8)]
    for copy in copies:
        copy.start()
    copies[0].wait()
    state = here[0]
    for k in range(PLANES):
        x, y = divmod(k, NY)
        field[k] = jnp.concatenate([state[:, x, y, :], jnp.zeros((NS, LANES - NZ), F32)], axis=1)
    put_faces(field, *faces)
    for copy in copies[1:]:
        copy.wait()
    setup(*here[1:], *tables, fzt_pad)


def source(c_state, c_now, state, field, wt, bar, stoich, base, inverse):
    inverse[...] = 1.0 / (1.5 + jnp.tanh(field[:, 0, :]))
    cells = jnp.concatenate([field[k] for k in range(PLANES)], axis=1)
    speed = lax.dot_general(wt[...], cells, (((0,), (0,)), ((), ())), precision=HIGH, preferred_element_type=F32)
    heat = jnp.concatenate(
        [jnp.exp(bar[...] * jnp.broadcast_to(inverse[k : k + 1, :], (NR, LANES))) for k in range(PLANES)], axis=1
    )
    made = jnp.dot(stoich[...], speed * heat, precision=HIGH, preferred_element_type=F32)
    for k in range(PLANES):
        value = c_now * (field[k] + made[:, k * LANES : (k + 1) * LANES])
        if state is not None:
            value = value + c_state * state[k]
        base[k] = value


def source_kernel(rates, *refs):
    state, *rest = refs if rates[0] else (None, *refs)
    source(*rates, state, *rest)


def scale_of(rows):
    return jnp.exp(0.7 * jnp.log((1.5 + jnp.tanh(rows)) / 2.5))


def advance(c_now, base, field, diff, x_first, y_first, z_first, y_second, x_second, z_second, x_halo, y_halo, z_halo, full, own_k, side_k, emit):
    odd_x, odd_y, odd_z = parity("gx"), parity("gy"), parity("gz")
    for i in range(8):
        x_halo[8 * (1 - odd_x) + i] = x_first[i]
        x_halo[8 * odd_x + i] = x_second[i]
        y_halo[8 * (1 - odd_y) + i] = y_first[i]
        y_halo[8 * odd_y + i] = y_second[i]
    z_halo[1 - odd_z] = z_first[...]
    z_halo[odd_z] = z_second[...]
    lane = lanes_of((NS, LANES))
    z_ends = jnp.where(lane % 8 < 2, pltpu.roll(z_halo[1], LANES - 6, 1), pltpu.roll(z_halo[0], 2, 1))
    for k in range(PLANES):
        full[k] = jnp.where(lane < NZ, field[k], pltpu.roll(z_ends, (NZ - 8 * k) % LANES, 1))
    own_k[...] = scale_of(full[:, 0, :])
    for i in range(4):
        side_k[i : i + 1, :] = x_halo[4 + i, 0:1, :]
        side_k[4 + i : 5 + i, :] = x_halo[8 + i, 0:1, :]
        side_k[8 + i : 9 + i, :] = y_halo[2 * i + 1, 0:1, :]
        side_k[12 + i : 13 + i, :] = y_halo[8 + 2 * i, 0:1, :]
    side_k[...] = scale_of(side_k[...])
    weight = c_now * diff[...]

    def wide(row):
        return jnp.broadcast_to(row, (NS, LANES))

    def k_at(x, y):
        if x < 0:
            return wide(side_k[y : y + 1, :])
        if x >= NX:
            return wide(side_k[4 + y : 5 + y, :])
        if y < 0:
            return wide(side_k[8 + x : 9 + x, :])
        if y >= NY:
            return wide(side_k[12 + x : 13 + x, :])
        k = x * NY + y
        return wide(own_k[k : k + 1, :])

    def y_at(x, y):
        if x < 0:
            return x_halo[(x + 2) * NY + y]
        if x >= NX:
            return x_halo[8 + (x - NX) * NY + y]
        if y < 0:
            return y_halo[x * 2 + y + 2]
        if y >= NY:
            return y_halo[8 + x * 2 + y - NY]
        return full[x * NY + y]

    for k in range(PLANES):
        x, y = divmod(k, NY)
        here = full[k]
        total = k_at(x + 1, y) * (y_at(x + 2, y) - here) - k_at(x - 1, y) * (here - y_at(x - 2, y))
        total = total + (k_at(x, y + 1) * (y_at(x, y + 2) - here) - k_at(x, y - 1) * (here - y_at(x, y - 2)))
        row = own_k[k : k + 1, :]
        after = wide(pltpu.roll(row, LANES - 1, 1))
        before = wide(pltpu.roll(row, 1, 1))
        total = total + (after * (pltpu.roll(here, LANES - 2, 1) - here) - before * (here - pltpu.roll(here, 2, 1)))
        emit(k, base[k] + weight * total)


def section_kernel(c_now, *refs):
    ins, (field, *faces), scratch = refs[:9], refs[9:15], refs[15:]

    def emit(k, plane):
        field[k] = plane

    advance(c_now, *ins, *scratch, emit)
    put_faces(field, *faces)


def last_kernel(c_now, *refs):
    ins, (fz, fy), (advanced, parts), scratch = refs[:9], refs[9:11], refs[11:13], refs[13:19]
    rows = refs[19]
    lane = lanes_of((NS, LANES))

    def emit(k, plane):
        x, y = divmod(k, NY)
        advanced[:, x, y, :] = plane[:, :NZ]
        rows[k * NS : (k + 1) * NS, :] = jnp.where(lane < NZ, plane, 0.0)

    advance(c_now, *ins, *scratch, emit)
    along_z = jnp.dot(rows[...], fz[...], precision=HIGH, preferred_element_type=F32)
    n_z = fz.shape[1] // LANES
    n_y = fy.shape[1] // LANES
    for g in range(n_z):
        by_y = []
        for y in range(NY):
            value = along_z[y * NS : (y + 1) * NS, g * LANES : (g + 1) * LANES]
            for x in range(1, NX):
                k = x * NY + y
                value = jnp.where(
                    lane // 32 == x, along_z[k * NS : (k + 1) * NS, g * LANES : (g + 1) * LANES], value
                )
            by_y.append(value)
        for j in range(n_y):
            total = fy[0:1, j * LANES : (j + 1) * LANES] * by_y[0]
            for y in range(1, NY):
                total = total + fy[y : y + 1, j * LANES : (j + 1) * LANES] * by_y[y]
            parts[j * n_z + g] = total


def middle_kernel(factor_x, parts, out):
    count = parts.shape[0]
    terms = [parts[i] for i in range(count)]
    while len(terms) > 1:
        terms = [terms[i] + terms[i + 1] for i in range(0, len(terms), 2)]
    total = terms[0]
    lane = lanes_of((4, LANES))
    by_x = []
    for x in range(NX):
        value = jnp.zeros((4, LANES), F32)
        for low in range(4):
            rolled = total[4 * low : 4 * low + 4, :]
            if low != x:
                rolled = pltpu.roll(rolled, (32 * (low - x)) % LANES, 1)
            value = jnp.where(lane // 32 == low, rolled, value)
        by_x.append(value)
    for a in range(out.shape[0]):
        value = factor_x[0, a] * by_x[0]
        for x in range(1, NX):
            value = value + factor_x[x, a] * by_x[x]
        out[a] = value


def final_kernel(parts, out, rows):
    count = parts.shape[0]
    terms = [parts[i] for i in range(count)]
    while len(terms) > 1:
        terms = [terms[i] + terms[i + 1] for i in range(0, len(terms), 2)]
    total = terms[0]
    for low in range(4):
        piece = total if low == 0 else pltpu.roll(total, LANES - 32 * low, 1)
        rows[4 * low : 4 * low + 4, :] = piece
    turned = jnp.transpose(rows[...])
    for b in range(NB):
        out[0, b] = turned[b * NC : (b + 1) * NC, :]


def swapped(faces):
    x_first, x_second, y_first, y_second, packed = faces

    def swap(value, axis, start):
        pairs = []
        for i in range(start, lax.axis_size(axis) - 1, 2):
            pairs += [(i, i + 1), (i + 1, i)]
        return lax.ppermute(value, axis, pairs)

    y_second = swap(y_second, "gy", 1)
    y_first = swap(y_first, "gy", 0)
    x_first = swap(x_first, "gx", 0)
    x_second = swap(x_second, "gx", 1)
    z_second = swap(packed, "gz", 1)
    z_first = swap(packed, "gz", 0)
    return x_first, y_first, z_first, y_second, x_second, z_second


HALO_SCRATCH = [
    pltpu.VMEM(FIELD, F32),
    pltpu.VMEM(FIELD, F32),
    pltpu.VMEM((2, NS, LANES), F32),
    pltpu.VMEM(FIELD, F32),
    pltpu.VMEM((PLANES, LANES), F32),
    pltpu.VMEM((16, LANES), F32),
]
FACES = [shaped(*FIELD), shaped(*FACE), shaped(*FACE), shaped(*FACE), shaped(*FACE), shaped(NS, LANES)]


def kernel(body, name, outs, scalars, arrays, scratch=()):
    single = not isinstance(outs, list)
    return pl.pallas_call(
        body,
        name=name,
        out_shape=outs,
        in_specs=smem(scalars) + vmem(arrays),
        out_specs=vmem(1)[0] if single else vmem(len(outs)),
        scratch_shapes=list(scratch),
        compiler_params=pltpu.CompilerParams(vmem_limit_bytes=8 * 1024 * 1024),
    )


def local(state_grid, diffusivity, prefactor_list, arrhenius_barrier, w_react, stoich_matrix, factor_x, factor_y, factor_z):
    n_x, n_y, n_z = (lax.axis_size(axis) for axis in ("gx", "gy", "gz"))
    inverse = pltpu.VMEM((PLANES, LANES), F32)
    tables = [shaped(NS, NR), shaped(NS, NR), shaped(NS, LANES), shaped(NR, LANES), shaped(LANES, n_z * LANES), shaped(NY, n_y * LANES)]
    ins = (state_grid, diffusivity, prefactor_list, arrhenius_barrier, w_react.T, stoich_matrix, factor_y, factor_z.T)
    entered = pl.pallas_call(
        enter_kernel,
        name="enter",
        out_shape=FACES + tables,
        in_specs=[pl.BlockSpec(memory_space=pltpu.HBM)] * len(ins),
        out_specs=vmem(12),
        scratch_shapes=[pltpu.VMEM((factor_z.shape[1], LANES), F32)]
        + [pltpu.VMEM(value.shape, F32) for value in ins]
        + [pltpu.SemaphoreType.DMA((len(ins),))],
        compiler_params=pltpu.CompilerParams(vmem_limit_bytes=8 * 1024 * 1024),
    )(*(pltpu.with_memory_space_constraint(value, pltpu.HBM) for value in ins))
    state, faces, (wt, stoich, diff, bar, fz, fy) = entered[0], entered[1:6], entered[6:]

    def section(c_now, base, field, halos):
        body = lambda *refs: section_kernel(c_now, *refs)
        return kernel(body, "section", FACES, 0, 9, HALO_SCRATCH)(base, field, diff, *halos)

    def base_of(c_state, c_now, field):
        body = lambda *refs: source_kernel((c_state, c_now), *refs)
        ins = ([state] if c_state else []) + [field, wt, bar, stoich]
        return kernel(body, "source", shaped(*FIELD), 0, len(ins), [inverse])(*ins)

    field = state
    for c_state, c_now in ((0.0, 1.0), (0.75, 0.25)):
        halos = swapped(faces)
        field, *faces = section(c_now, base_of(c_state, c_now, field), field, halos)
    halos = swapped(faces)
    base = base_of(1.0 / 3.0, 2.0 / 3.0, field)
    advanced, parts = kernel(
        lambda *refs: last_kernel(2.0 / 3.0, *refs),
        "last",
        [shaped(NS, NX, NY, NZ), shaped(n_y * n_z, NS, LANES)],
        0,
        11,
        HALO_SCRATCH + [pltpu.VMEM((PLANES * NS, LANES), F32)],
    )(base, field, diff, *halos, fz, fy)
    parts = lax.all_to_all(parts, ("gy", "gz"), 0, 0, tiled=True)
    parts = kernel(middle_kernel, "middle", shaped(n_x, 4, LANES), 1, 1)(factor_x, parts)
    parts = lax.all_to_all(parts, "gx", 0, 0, tiled=True)
    tucker_core = kernel(final_kernel, "final", shaped(1, NB, NC, NS), 0, 1, [pltpu.VMEM((NS, LANES), F32)])(parts)
    return advanced, tucker_core


def solution(mesh):
    placed = (P(None, "gx", "gy", "gz"), P(), P(), P(), P(), P(), P("gx", None), P("gy", None), P("gz", None))
    return jax.shard_map(
        local,
        mesh=mesh,
        in_specs=placed,
        out_specs=(P(None, "gx", "gy", "gz"), P("gx", "gy", "gz", None)),
        check_vma=False,
    )
```
